32 devices in a mesh: bl: 4 (over y, x), freq: 8 (over z, core).
Axes of the slice: x: 2, y: 2, z: 4, core: 2. Of those that a mesh axis runs over, the one named last changes fastest.
Arguments:
- visibilities: float32 [2, 2, 128, 8192], P(None, None, 'freq', 'bl'), may hold values from -8 to 8
- sample_flag_weight: int32 [2, 128, 8192], P(None, 'freq', 'bl'), may hold values from 0 to 4
- baseline_station_pair: int32 [2, 8192], P(None, 'bl'), may hold values from 0 to 511, as said below
- baseline_spatial_coords: float32 [2, 2, 8192], P(None, None, 'bl'), may hold values from -6 to 6
- directions: float32 [2, 8], replicated, may hold values from -0.5 to 0.5
- source_flux: float32 [8, 128], P(None, 'freq'), may hold values from 0.5 to 2
- channel_ratio: float32 [128], P('freq'), may hold values from 0.7 to 1.4
- jones_gains: float32 [2, 8, 128, 512], P(None, None, 'freq'), may hold values from -4 to 4
- scaled_dual: float32 [2, 8, 128, 512], P(None, None, 'freq'), may hold values from -2 to 2
- consensus: float32 [2, 3, 8, 512], replicated, may hold values from -3 to 3
- penalty: float32 [8], replicated, may hold values from 0.3 to 3
Outputs:
- new_gains: float32 [2, 8, 128, 512], P(None, None, 'freq')
- new_consensus: float32 [2, 3, 8, 512], replicated
- new_dual: float32 [2, 8, 128, 512], P(None, None, 'freq')
- residuals: float32 [2, 2, 128, 8192], P(None, None, 'freq', 'bl')
The draws below stay inside these ranges and needn't reach their ends.
Inputs may be any that keep to these rules, and one draw needn't show every extreme that they name: `baseline_station_pair`: the two stations of every baseline differ.
All inputs are finite; a program needn't handle non-finite values.
Results may differ from the reference program's by a relative error of at most 0.00016.
Values sent between devices are 32-bit elements; how exact they have to be, the bound alone decides.
A program may use at most 64 MiB of HBM per device.

```python
import math
import jax
import jax.numpy as jnp
from jax import lax

STATION_TOTAL = 512
DIRS = 8
NPOLY = 3
ITERS = 3
TIME_SLOT_TOTAL = 2
BASELINE_TOTAL = 8192
CHANNEL_TOTAL = 128


def draw_baseline_station_pair(key, part):
    leading_dims = jax.random.randint(jax.random.fold_in(key, 11), (BASELINE_TOTAL,), 0, STATION_TOTAL)
    update_step_length = jax.random.randint(jax.random.fold_in(key, 12), (BASELINE_TOTAL,), 1, STATION_TOTAL)
    return jnp.stack([leading_dims, (leading_dims + update_step_length) % STATION_TOTAL]).astype(jnp.int32)


def set_ends(result, own_key, low, high):
    spot = [jax.random.randint(jax.random.fold_in(own_key, axis), (), 0, length) for axis, length in enumerate(result.shape)]
    widest = result.shape.index(max(result.shape))
    neighbour = spot[:widest] + [(spot[widest] + 1) % result.shape[widest]] + spot[widest + 1:]
    return result.at[tuple(spot)].set(low).at[tuple(neighbour)].set(high)


def level_of(key, dims, cuts, low, top_value):
    gain = 1.0
    for dim, shards_of in cuts:
        draws = jax.random.uniform(jax.random.fold_in(jax.random.fold_in(key, 6), dim), (shards_of,), jnp.float32, low / len(cuts), top_value / len(cuts))
        gain = gain * jnp.repeat(jnp.exp(draws), dims[dim] // shards_of).reshape((-1,) + (1,) * (len(dims) - 1 - dim))
    return gain


def gaussian(own_key, dims, spread, reach, cuts=(), held_as=jnp.bfloat16):
    values = jax.random.normal(own_key, dims, jnp.float32) * spread
    if len(cuts) > 0:
        values = level_of(own_key, dims, cuts, -0.22, 0.18) * values
    return jnp.clip(values, min=-reach, max=reach).astype(held_as)


def setup_inputs(seed: int = 0) -> dict:
    arg_keys = jax.random.split(jax.random.key(seed), 12)
    return {
        "visibilities": gaussian(arg_keys[0], (2, TIME_SLOT_TOTAL, CHANNEL_TOTAL, BASELINE_TOTAL), 1.0, 8.0, ((2, 8), (3, 4)), jnp.float32),
        "sample_flag_weight": set_ends(jax.random.randint(arg_keys[1], (TIME_SLOT_TOTAL, CHANNEL_TOTAL, BASELINE_TOTAL), 0, 5), jax.random.fold_in(arg_keys[1], 1), 0, 4).astype(jnp.int32),
        "baseline_station_pair": draw_baseline_station_pair(jax.random.fold_in(arg_keys[11], 71), 0),
        "baseline_spatial_coords": gaussian(arg_keys[3], (2, TIME_SLOT_TOTAL, BASELINE_TOTAL), 1.0, 6.0, ((2, 4),), jnp.float32),
        "directions": jnp.clip(jax.random.uniform(arg_keys[4], (2, DIRS), jnp.float32, -0.5, 0.5), -0.5, 0.5),
        "source_flux": jnp.clip(jnp.exp(math.log(2.0) - 1.3862944 * jax.random.uniform(arg_keys[5], (DIRS, CHANNEL_TOTAL), jnp.float32) ** level_of(arg_keys[5], (DIRS, CHANNEL_TOTAL), ((1, 8),), -0.2, 0.2)), 0.5, 2.0),
        "channel_ratio": jnp.clip(jnp.exp(math.log(1.4) - 0.6931472 * jax.random.uniform(arg_keys[6], (CHANNEL_TOTAL,), jnp.float32) ** level_of(arg_keys[6], (CHANNEL_TOTAL,), ((0, 8),), -0.2, 0.2)), 0.7, 1.4),
        "jones_gains": gaussian(arg_keys[7], (2, DIRS, CHANNEL_TOTAL, STATION_TOTAL), 0.8, 4.0, ((2, 8),), jnp.float32),
        "scaled_dual": gaussian(arg_keys[8], (2, DIRS, CHANNEL_TOTAL, STATION_TOTAL), 0.3, 2.0, ((2, 8),), jnp.float32),
        "consensus": gaussian(arg_keys[9], (2, NPOLY, DIRS, STATION_TOTAL), 0.5, 3.0, (), jnp.float32),
        "penalty": jnp.clip(jnp.exp(jax.random.uniform(arg_keys[10], (DIRS,), jnp.float32, math.log(0.3), math.log(3.0))), 0.3, 3.0),
    }


robust_dof = 2.0
small_term = 1e-06
two_pi = 2.0 * math.pi

def legendre(ratios):
    scaled = (ratios - 1.05) / 0.35
    values = [jnp.ones_like(scaled), scaled]
    for degree in range(1, NPOLY - 1):
        values.append(((2 * degree + 1) * scaled * values[degree] - degree * values[degree - 1]) / (degree + 1))
    return jnp.stack(values[:NPOLY])

def coherency(coords, sky_dirs, fluxes, ratios):
    project = sky_dirs[0][:, None, None] * coords[0][None] + sky_dirs[1][:, None, None] * coords[1][None]
    phases = two_pi * project[:, :, None, :] * ratios[None, None, :, None]
    amplitude = fluxes[:, None, :, None]
    return (amplitude * jnp.cos(phases), amplitude * jnp.sin(phases))

def predict(gain_re, gain_im, pair_index, sky_re, sky_im):
    left_re = jnp.take(gain_re, pair_index[0], axis=2)
    left_im = jnp.take(gain_im, pair_index[0], axis=2)
    right_re = jnp.take(gain_re, pair_index[1], axis=2)
    right_im = jnp.take(gain_im, pair_index[1], axis=2)
    pair_re = left_re * right_re + left_im * right_im
    pair_im = left_im * right_re - left_re * right_im
    model_re = pair_re[:, None] * sky_re - pair_im[:, None] * sky_im
    model_im = pair_re[:, None] * sky_im + pair_im[:, None] * sky_re
    return ((left_re, left_im, right_re, right_im), model_re, model_im)

def residual_of(observed, model_re, model_im):
    return (observed[0] - jnp.sum(model_re, axis=0), observed[1] - jnp.sum(model_im, axis=0))

def robust_weights(flagged, error_re, error_im, sigma_sq):
    return flagged * (robust_dof + 1.0) / (robust_dof + (error_re * error_re + error_im * error_im) / sigma_sq)

def normal_terms(error_re, error_im, model_re, model_im, weights, sky_re, sky_im, side_gains, pair_index, station_list):
    target_re = error_re[None] + model_re
    target_im = error_im[None] + model_im
    cross_re = sky_re * target_re + sky_im * target_im
    cross_im = sky_re * target_im - sky_im * target_re
    weight_wide = weights[None]
    summed_re = jnp.sum(weight_wide * cross_re, axis=1)
    summed_im = jnp.sum(weight_wide * cross_im, axis=1)
    powers = jnp.sum(weight_wide * (sky_re * sky_re + sky_im * sky_im), axis=1)
    left_re, left_im, right_re, right_im = side_gains
    first_re = right_re * summed_re - right_im * summed_im
    first_im = right_re * summed_im + right_im * summed_re
    second_re = left_re * summed_re + left_im * summed_im
    second_im = left_im * summed_re - left_re * summed_im
    first_norm = (right_re * right_re + right_im * right_im) * powers
    second_norm = (left_re * left_re + left_im * left_im) * powers
    stacked_first = jnp.stack([first_re, first_im, first_norm])
    stacked_second = jnp.stack([second_re, second_im, second_norm])
    zeroed = jnp.zeros(stacked_first.shape[:3] + (station_list,), stacked_first.dtype)
    return zeroed.at[:, :, :, pair_index[0]].add(stacked_first).at[:, :, :, pair_index[1]].add(stacked_second)

def update_gains(gain_re, gain_im, normal_sums, anchor_re, anchor_im, effective_penalty):
    penalty_wide = effective_penalty[:, None, None]
    divisor = normal_sums[2] + penalty_wide
    solved_re = (normal_sums[0] + penalty_wide * anchor_re) / divisor
    solved_im = (normal_sums[1] + penalty_wide * anchor_im) / divisor
    return (0.5 * (gain_re + solved_re), 0.5 * (gain_im + solved_im))

def cholesky_solve(gram_total, flat_rhs):
    factor = jnp.linalg.cholesky(gram_total)
    matrix_order = gram_total.shape[0]
    forward = []
    for row_index in range(matrix_order):
        running = flat_rhs[row_index]
        for col_index in range(row_index):
            running = running - factor[row_index, col_index] * forward[col_index]
        forward.append(running / factor[row_index, row_index])
    backward = [None] * matrix_order
    for row_index in reversed(range(matrix_order)):
        running = forward[row_index]
        for col_index in range(row_index + 1, matrix_order):
            running = running - factor[col_index, row_index] * backward[col_index]
        backward[row_index] = running / factor[row_index, row_index]
    return jnp.stack(backward)

def solve_consensus(gram_total, rhs_total):
    matrix_order = gram_total.shape[0]
    flat_rhs = jnp.moveaxis(rhs_total, 1, 0).reshape(matrix_order, -1)
    solved = cholesky_solve(gram_total, flat_rhs)
    return jnp.moveaxis(solved.reshape((matrix_order, rhs_total.shape[0]) + rhs_total.shape[2:]), 0, 1)

def reference(visibilities, sample_flag_weight, baseline_station_pair, baseline_spatial_coords, directions, source_flux, channel_ratio, jones_gains, scaled_dual, consensus, penalty):
    chan_block = math.gcd(CHANNEL_TOTAL, 8)
    blocks = CHANNEL_TOTAL // chan_block

    def split_axis(tensor, position):
        old_shape = tensor.shape
        reshaped = tensor.reshape(old_shape[:position] + (blocks, chan_block) + old_shape[position + 1:])
        return jnp.moveaxis(reshaped, position, 0)

    def join_axis(tensor, position):
        moved_axes = jnp.moveaxis(tensor, 0, position)
        old_shape = moved_axes.shape
        return moved_axes.reshape(old_shape[:position] + (blocks * chan_block,) + old_shape[position + 2:])
    effective_penalty = penalty * (2.0 * BASELINE_TOTAL * TIME_SLOT_TOTAL / STATION_TOTAL)
    poly_basis = legendre(channel_ratio)
    anchor = jnp.einsum('jc,xjks->xkcs', poly_basis, consensus, precision=lax.Precision.HIGHEST) - scaled_dual
    flagged = sample_flag_weight.astype(jnp.float32)
    weight_count = jnp.sum(flagged)
    vis_blocks = split_axis(visibilities, 2)
    flag_blocks = split_axis(flagged, 1)
    flux_blocks = split_axis(source_flux, 1)
    ratio_blocks = channel_ratio.reshape(blocks, chan_block)
    anchor_blocks = split_axis(anchor, 2)

    def block_model(gain_block, flux_block, ratio_block):
        sky_re, sky_im = coherency(baseline_spatial_coords, directions, flux_block, ratio_block)
        side_gains, model_re, model_im = predict(gain_block[0], gain_block[1], baseline_station_pair, sky_re, sky_im)
        return (sky_re, sky_im, side_gains, model_re, model_im)
    gain_state = jones_gains
    for iteration in range(ITERS):
        gain_blocks = split_axis(gain_state, 2)

        def misfit_block(block_items):
            vis_block, flag_block, flux_block, ratio_block, gain_block = block_items
            sky_re, sky_im, side_gains, model_re, model_im = block_model(gain_block, flux_block, ratio_block)
            error_re, error_im = residual_of(vis_block, model_re, model_im)
            return jnp.sum(flag_block * (error_re * error_re + error_im * error_im))
        squares = jnp.sum(lax.map(misfit_block, (vis_blocks, flag_blocks, flux_blocks, ratio_blocks, gain_blocks)))
        sigma_sq = squares / (weight_count + 1.0) + small_term

        def update_block(block_items):
            vis_block, flag_block, flux_block, ratio_block, gain_block, anchor_block = block_items
            sky_re, sky_im, side_gains, model_re, model_im = block_model(gain_block, flux_block, ratio_block)
            error_re, error_im = residual_of(vis_block, model_re, model_im)
            weights = robust_weights(flag_block, error_re, error_im, sigma_sq)
            normal_sums = normal_terms(error_re, error_im, model_re, model_im, weights, sky_re, sky_im, side_gains, baseline_station_pair, STATION_TOTAL)
            new_re, new_im = update_gains(gain_block[0], gain_block[1], normal_sums, anchor_block[0], anchor_block[1], effective_penalty)
            return jnp.stack([new_re, new_im])
        gain_state = join_axis(lax.map(update_block, (vis_blocks, flag_blocks, flux_blocks, ratio_blocks, gain_blocks, anchor_blocks)), 2)
    final_blocks = split_axis(gain_state, 2)

    def residual_block(block_items):
        vis_block, flux_block, ratio_block, gain_block = block_items
        sky_re, sky_im, side_gains, model_re, model_im = block_model(gain_block, flux_block, ratio_block)
        error_re, error_im = residual_of(vis_block, model_re, model_im)
        return jnp.stack([error_re, error_im])
    residuals = join_axis(lax.map(residual_block, (vis_blocks, flux_blocks, ratio_blocks, final_blocks)), 2)
    gram_total = jnp.dot(poly_basis, poly_basis.T, precision=lax.Precision.HIGHEST)
    rhs_total = jnp.einsum('jc,xkcs->xjks', poly_basis, gain_state + scaled_dual, precision=lax.Precision.HIGHEST)
    new_consensus = solve_consensus(gram_total, rhs_total)
    new_dual = scaled_dual + gain_state - jnp.einsum('jc,xjks->xkcs', poly_basis, new_consensus, precision=lax.Precision.HIGHEST)
    return (gain_state, new_consensus, new_dual, residuals)
```

```python
import functools
import math

import jax
import jax.numpy as jnp
from jax import lax
from jax.experimental import pallas as pl
from jax.experimental.pallas import tpu as pltpu
from jax.sharding import PartitionSpec as P

NPOLY = 3
ITERS = 3

robust_dof = 2.0
small_term = 1e-06
two_pi = 2.0 * math.pi
MESH = pl.DeviceIdType.MESH
f32, bf16, i32 = jnp.float32, jnp.bfloat16, jnp.int32

SIN_TERMS = [(-1.0) ** n * two_pi ** (2 * n + 1) / math.factorial(2 * n + 1) for n in range(6)]
COS_TERMS = [(-1.0) ** n * two_pi ** (2 * n) / math.factorial(2 * n) for n in range(7)]
GRAMS = [(a, b) for a in range(NPOLY) for b in range(a + 1)]


def horner(terms, square):
    value = jnp.full_like(square, terms[-1])
    for term in terms[-2::-1]:
        value = value * square + term
    return value


def turn_parts(turns):
    half = jnp.floor(turns * 2.0 + 0.5)
    rest = turns - half * 0.5
    sign = 1.0 - 2.0 * (half - 2.0 * jnp.floor(half * 0.5))
    square = rest * rest
    return horner(COS_TERMS, square), rest * horner(SIN_TERMS, square), sign


def split_two(value):
    high = value.astype(bf16)
    low = (value - high.astype(f32)).astype(bf16)
    return high, low


def legendre(ratio):
    scaled = (ratio - 1.05) / 0.35
    return [jnp.ones_like(scaled), scaled, (3.0 * scaled * scaled - 1.0) / 2.0]


def kernel(
    sizes,
    vis,
    flag,
    pair,
    coords,
    dirs,
    flux,
    ratio,
    gains_in,
    dual,
    cons_in,
    penalty,
    gains_out,
    cons_out,
    dual_out,
    resid_out,
    table,
    meta,
    sendx,
    xin,
    sky,
    sky_own,
    const,
    const_own,
    anchor,
    side,
    gsplit,
    gcur,
    visd,
    flagd,
    err,
    stacked,
    acc,
    gall,
    resbuf,
    sbuf,
    rhs,
    rsum,
    solved,
    coef,
    m_send,
    m_recv,
    x_send,
    x_recv,
    s_send,
    s_recv,
    g_send,
    g_recv,
    c_send,
    c_recv,
):
    nb, nf, slots, chans, base, dirn, stations, rho_scale = sizes
    fl = chans // nb
    rows = dirn * fl
    units = rows // 16
    total = base * nb
    kp = 8 // fl
    ndev = nb * nf
    half = 128 * (-(-3 * rows // 128))
    lanes = stations // 128
    chunks = dirn * lanes
    ch = min(1024, base)
    me = lax.axis_index("bl")
    mf = lax.axis_index("freq")
    ident = me * nf + mf

    def bl_peer(o):
        return lax.bitwise_xor(me, o)

    def any_peer(o):
        return {"bl": lax.bitwise_xor(me, o // nf), "freq": lax.bitwise_xor(mf, o % nf)}

    def remote(src, dst, send, recv, device):
        return pltpu.make_async_remote_copy(
            src_ref=src, dst_ref=dst, send_sem=send, recv_sem=recv,
            device_id=device, device_id_type=MESH,
        )

    barrier = pltpu.get_barrier_semaphore()
    for o in range(1, ndev):
        pl.semaphore_signal(barrier, inc=1, device_id=any_peer(o), device_id_type=MESH)

    meta[me, 0:2] = pair[...].astype(f32)
    for c in range(2):
        for t in range(slots):
            meta[me, 2 + c * slots + t : 3 + c * slots + t] = coords[c, t : t + 1]
    for g in range(nb):
        own = slice(g * fl, (g + 1) * fl)
        for t in range(slots):
            for c in range(2):
                at = (c * slots + t) * fl
                sendx[g, at : at + fl] = vis[c, t, own]
            at = (2 * slots + t) * fl
            sendx[g, at : at + fl] = flag[t, own].astype(f32)
    xin[me] = sendx[me]

    row = lax.broadcasted_iota(i32, (rows, 128), 0)
    row_k, row_f = row // fl, row % fl

    def by(index, count, pick):
        value = jnp.full(index.shape, pick(0), f32)
        for n in range(1, count):
            value = jnp.where(index == n, pick(n), value)
        return value

    const[0] = by(row_k, dirn, lambda k: dirs[0, k])
    const[1] = by(row_k, dirn, lambda k: dirs[1, k])
    const[2] = by(row_k, dirn, lambda k: penalty[k]) * rho_scale
    for g in range(nb):
        const_own[g, 0] = by(row_f, fl, lambda f: ratio[0, g * fl + f])
        const_own[g, 1] = by(row, rows, lambda r: flux[r // fl, g * fl + r % fl])
    const[3] = const_own[me, 1] * const_own[me, 1]

    def build_table(g):
        iota = lax.broadcasted_iota(i32, (stations, 256), 0)

        def step(i, carry):
            at = pl.multiple_of(i * 256, 256)
            for s in range(2):
                hit = iota == meta[g, s : s + 1, pl.ds(at, 256)].astype(i32)
                where = pl.ds(pl.multiple_of(s * total + g * base + at, 256), 256)
                table[:, where] = jnp.where(hit, 1.0, 0.0).astype(bf16)
            return carry

        lax.fori_loop(0, base // 256, step, 0)

    def build_sky(g, coord, put):
        def step(i, carry):
            cols = pl.ds(pl.multiple_of(i * 128, 128), 128)
            for t in range(slots):
                u, v = coord(t, cols)
                for w in range(units):
                    at = slice(w * 16, (w + 1) * 16)
                    project = const[0, at] * u + const[1, at] * v
                    cosine, sine, sign = turn_parts(project * const_own[g, 0, at])
                    amplitude = sign * const_own[g, 1, at]
                    put(t, at, i, amplitude * cosine, amplitude * sine)
            return carry

        lax.fori_loop(0, base // 128, step, 0)

    def setup(g):
        build_table(g)

        def coord(t, cols):
            return meta[g, 2 + t : 3 + t, cols], meta[g, 2 + slots + t : 3 + slots + t, cols]

        def put(t, at, i, re, im):
            cols = pl.ds(pl.multiple_of(g * base + i * 128, 128), 128)
            sky[0, t, at, cols] = re
            sky[1, t, at, cols] = im

        build_sky(me, coord, put)

    pl.semaphore_wait(barrier, ndev - 1)
    firsts = [
        remote(meta.at[me], meta.at[me], m_send.at[o], m_recv.at[o], {"bl": bl_peer(o)})
        for o in range(1, nb)
    ]
    seconds = [
        remote(sendx.at[bl_peer(o)], xin.at[me], x_send.at[o], x_recv.at[o], {"bl": bl_peer(o)})
        for o in range(1, nb)
    ]
    for copy in firsts + seconds:
        copy.start()
    setup(me)

    lane = lax.broadcasted_iota(i32, (1, 128), 1)
    gram_row = jnp.zeros((1, 128), f32)
    for n, (a, b) in enumerate(GRAMS):
        entry = jnp.zeros((1, 128), f32)
        for f in range(fl):
            basis = legendre(jnp.full((1, 128), ratio[0, me * fl + f], f32))
            entry = entry + basis[a] * basis[b]
        gram_row = gram_row + jnp.where(lane == n, entry, 0.0)
    for it in range(ITERS):
        sbuf[it, 0, 2:3] = gram_row
        sbuf[it, 0, 3:4] = jnp.zeros((1, 128), f32)

    def wide(column):
        return jnp.broadcast_to(column[:, :1], (rows, stations))

    def own_rows(ref, c, k):
        value = ref[c, k, 0:fl]
        for g in range(1, nb):
            value = jnp.where(me == g, ref[c, k, g * fl : (g + 1) * fl], value)
        return value

    basis_rows = legendre(const_own[me, 0])
    for c in range(2):
        for k in range(dirn):
            at = k * fl
            gcur[c * rows + at : c * rows + at + fl] = own_rows(gains_in, c, k)
            value = -own_rows(dual, c, k)
            for j in range(NPOLY):
                weight = basis_rows[j][at : at + fl, :1]
                value = value + weight * cons_in[c, j, k : k + 1]
            anchor[c * rows + at : c * rows + at + fl] = value * const[2, at : at + fl, :1]
    stacked[...] = jnp.zeros_like(stacked)

    def put_split(slot, value):
        high, low = split_two(value)
        gsplit[slot, 0 : 2 * rows] = high
        gsplit[slot, 2 * rows : 4 * rows] = low

    put_split(0, gcur[...])
    for o in range(1, nb):
        firsts[o - 1].wait_recv()
        setup(bl_peer(o))

    def gather(slot, off, width):
        both = jnp.dot(
            gsplit[slot], table[:, pl.ds(off, width)], preferred_element_type=f32
        )
        return both[: 2 * rows] + both[2 * rows :]

    def fold(value):
        value = value[:8] + value[8:]
        shift = fl
        while shift < 8:
            value = value + pltpu.roll(value, shift, 0)
            shift *= 2
        return value

    def model(left, right, sub, field, cols):
        inside = slice(sub * 128, (sub + 1) * 128)
        real, imag = [None] * slots, [None] * slots
        for w in range(units):
            re, im = slice(w * 16, w * 16 + 16), slice(rows + w * 16, rows + w * 16 + 16)
            lr, li = left[re, inside], left[im, inside]
            rr, ri = right[re, inside], right[im, inside]
            pr = lr * rr + li * ri
            pi = li * rr - lr * ri
            for t in range(slots):
                sr, si = field(0, t, re, cols), field(1, t, re, cols)
                mr, mi = pr * sr - pi * si, pr * si + pi * sr
                real[t] = mr if w == 0 else real[t] + mr
                imag[t] = mi if w == 0 else imag[t] + mi
        return [fold(v) for v in real], [fold(v) for v in imag]

    def sky_all(c, t, at, cols):
        return sky[c, t, at, cols]

    def predict(observed):
        def step(i, misfit):
            at = pl.multiple_of(i * ch, ch)
            left = gather(0, at, ch)
            right = gather(0, pl.multiple_of(total + at, ch), ch)
            side[0, :, pl.ds(at, ch)] = left
            side[1, :, pl.ds(at, ch)] = right
            for sub in range(ch // 128):
                cols = pl.ds(pl.multiple_of(at + sub * 128, 128), 128)
                real, imag = model(left, right, sub, sky_all, cols)
                for t in range(slots):
                    if observed:
                        real[t] = visd[0, t, :, cols] - real[t]
                        imag[t] = visd[1, t, :, cols] - imag[t]
                        power = real[t] * real[t] + imag[t] * imag[t]
                        misfit = misfit + flagd[t, :, cols] * power
                    err[0, t, :, cols] = real[t]
                    err[1, t, :, cols] = imag[t]
            return misfit

        return lax.fori_loop(0, total // ch, step, jnp.zeros((8, 128), f32))

    def put_sum(it, at, value):
        sbuf[it, 0, at : at + 1] = jnp.sum(value, axis=0, keepdims=True) * (1.0 / kp)

    predict(False)
    for copy in seconds:
        copy.wait_recv()

    def spread_rows(value):
        return jnp.concatenate([value] * kp, axis=0)

    def observe():
        def outer(g, sums):
            def step(i, sums):
                misfit, count = sums
                here = pl.ds(pl.multiple_of(i * 128, 128), 128)
                cols = pl.ds(pl.multiple_of(g * base + i * 128, 128), 128)
                for t in range(slots):
                    at = (2 * slots + t) * fl
                    weight = spread_rows(xin[g, at : at + fl, here])
                    flagd[t, :, cols] = weight
                    count = count + weight
                    power = None
                    for c in range(2):
                        at = (c * slots + t) * fl
                        seen = spread_rows(xin[g, at : at + fl, here])
                        visd[c, t, :, cols] = seen
                        value = seen - err[c, t, :, cols]
                        err[c, t, :, cols] = value
                        power = value * value if c == 0 else power + value * value
                    misfit = misfit + weight * power
                return misfit, count

            return lax.fori_loop(0, base // 128, step, sums)

        zero = jnp.zeros((8, 128), f32)
        return lax.fori_loop(0, nb, outer, (zero, zero))

    def wait_all(ref, send, recv):
        return remote(ref, ref, send, recv, any_peer(1))

    def build_own_sky():
        for g in range(nb):
            def coord(t, cols):
                return coords[0, t : t + 1, cols], coords[1, t : t + 1, cols]

            def put(t, at, i, re, im, g=g):
                cols = pl.ds(pl.multiple_of(i * 128, 128), 128)
                sky_own[g, 0, t, at, cols] = re
                sky_own[g, 1, t, at, cols] = im

            build_sky(g, coord, put)

    def iteration(it, carry):
        @pl.when(it == 0)
        def _():
            misfit, count = observe()
            for n in range(ITERS):
                put_sum(n, 1, count)
            put_sum(it, 0, misfit)

        @pl.when(it > 0)
        def _():
            put_sum(it, 0, predict(True))

        for o in range(1, ndev):
            remote(
                sbuf.at[it, 0], sbuf.at[it, o], s_send.at[it], s_recv.at[it], any_peer(o)
            ).start()

        @pl.when(it == 0)
        def _():
            build_own_sky()

        finish = wait_all(sbuf.at[it, pl.ds(1, ndev - 1)], s_send.at[it], s_recv.at[it])
        finish.wait_recv()
        sums = jnp.sum(sbuf[it], axis=0)
        sums = jnp.sum(sums, axis=1, keepdims=True)
        sigma_sq = sums[0:1] / (sums[1:2] + 1.0) + small_term
        inverse = 1.0 / sigma_sq
        acc[...] = jnp.zeros_like(acc)

        def normal(i, carry):
            at = pl.multiple_of(i * ch, ch)
            for sub in range(ch // 128):
                cols = pl.ds(pl.multiple_of(at + sub * 128, 128), 128)
                weighted, wsum = [], None
                for t in range(slots):
                    er, ei = err[0, t, :, cols], err[1, t, :, cols]
                    power = er * er + ei * ei
                    r = flagd[t, :, cols] * (robust_dof + 1.0) / (robust_dof + power * inverse)
                    weighted.append([jnp.concatenate([r * e, r * e], axis=0) for e in (er, ei)])
                    wsum = r if t == 0 else wsum + r
                wsum = jnp.concatenate([wsum, wsum], axis=0)
                for w in range(units):
                    re, im = slice(w * 16, w * 16 + 16), slice(rows + w * 16, rows + w * 16 + 16)
                    lr, li = side[0, re, cols], side[0, im, cols]
                    rr, ri = side[1, re, cols], side[1, im, cols]
                    c2 = const[3, re] * wsum
                    xr = (lr * rr + li * ri) * c2
                    xi = (li * rr - lr * ri) * c2
                    for t in range(slots):
                        sr, si = sky[0, t, re, cols], sky[1, t, re, cols]
                        wr, wi = weighted[t]
                        xr = xr + (sr * wr + si * wi)
                        xi = xi + (sr * wi - si * wr)
                    terms = (
                        (rr * xr - ri * xi, lr * xr + li * xi),
                        (rr * xi + ri * xr, li * xr - lr * xi),
                        ((rr * rr + ri * ri) * c2, (lr * lr + li * li) * c2),
                    )
                    for q in range(3):
                        for s in range(2):
                            high, low = split_two(terms[q][s])
                            put = q * rows + w * 16
                            where = slice(s * ch + sub * 128, s * ch + sub * 128 + 128)
                            stacked[put : put + 16, where] = high
                            stacked[half + put : half + put + 16, where] = low
            for s in range(2):
                acc[...] += lax.dot_general(
                    table[:, pl.ds(pl.multiple_of(s * total + at, ch), ch)],
                    stacked[:, s * ch : (s + 1) * ch],
                    (((1,), (1,)), ((), ())),
                    preferred_element_type=f32,
                )
            return carry

        lax.fori_loop(0, total // ch, normal, 0)
        normals = (acc[:, :half] + acc[:, half:]).T
        divisor = 1.0 / (normals[2 * rows : 3 * rows] + wide(const[2]))
        for c in range(2):
            at = slice(c * rows, (c + 1) * rows)
            gcur[at] = 0.5 * (gcur[at] + (normals[at] + anchor[at]) * divisor)
        put_split(0, gcur[...])
        finish.wait_send()
        return carry

    lax.fori_loop(0, ITERS, iteration, 0)

    lanes_of = lax.broadcasted_iota(i32, (8 * dirn, 2 * rows), 1)
    rows_of = lax.broadcasted_iota(i32, (8 * dirn, 2 * rows), 0)
    ratio_lanes = by(lanes_of % fl, fl, lambda f: ratio[0, me * fl + f])
    basis = legendre(ratio_lanes)
    place = rows_of % 8
    weights = jnp.zeros((8 * dirn, 2 * rows), f32)
    for c in range(2):
        for j in range(NPOLY):
            hit = (place == c * NPOLY + j) & (lanes_of // rows == c)
            hit = hit & ((lanes_of % rows) // fl == rows_of // 8)
            weights = jnp.where(hit, basis[j], weights)
    both = []
    for c in range(2):
        for k in range(dirn):
            both.append(own_rows(dual, c, k))
    both = gcur[...] + jnp.concatenate(both, axis=0)
    rhs[...] = jnp.dot(
        weights, both, preferred_element_type=f32, precision=lax.Precision.HIGHEST
    )

    def tile(ref, n):
        return ref.at[
            pl.ds(pl.multiple_of((n // lanes) * 8, 8), 8),
            pl.ds(pl.multiple_of((n % lanes) * 128, 128), 128),
        ]

    def tile_value(ref, n):
        return ref[
            pl.ds(pl.multiple_of((n // lanes) * 8, 8), 8),
            pl.ds(pl.multiple_of((n % lanes) * 128, 128), 128),
        ]

    def owning(n, action):
        if ndev <= chunks:
            action()
        else:
            pl.when(n < chunks)(action)

    def ident_of(o):
        peer = any_peer(o)
        return peer["bl"] * nf + peer["freq"]

    for o in range(1, ndev):
        n = ident_of(o)

        def send(o=o, n=n):
            remote(
                tile(rhs, n), rsum.at[o], c_send.at[0], c_recv.at[0], any_peer(o)
            ).start()

        owning(n, send)

    gall[me] = gcur[...]
    spread = [
        remote(gall.at[me], gall.at[me], g_send.at[o], g_recv.at[o], {"bl": bl_peer(o)})
        for o in range(1, nb)
    ]
    for copy in spread:
        copy.start()

    def residual(o):
        g = bl_peer(o)
        if o > 0:
            spread[o - 1].wait_recv()
            put_split(0, gall[g])

        def sky_here(c, t, at, cols):
            return sky_own[g, c, t, at, cols]

        def step(i, carry):
            at = pl.multiple_of(i * ch, ch)
            off = me * base + at
            left = gather(0, pl.multiple_of(off, ch), ch)
            right = gather(0, pl.multiple_of(total + off, ch), ch)
            for sub in range(ch // 128):
                cols = pl.ds(pl.multiple_of(at + sub * 128, 128), 128)
                parts = model(left, right, sub, sky_here, cols)
                for c in range(2):
                    for t in range(slots):
                        put = (c * slots + t) * fl
                        resbuf[g, put : put + fl, cols] = (
                            sendx[g, put : put + fl, cols] - parts[c][t][:fl]
                        )
            return carry

        lax.fori_loop(0, base // ch, step, 0)

    residual(0)

    gram_total = jnp.sum(sbuf[0, :, 2:3], axis=0)
    gram = {
        ab: jnp.sum(jnp.where(lane == n, gram_total, 0.0), axis=1, keepdims=True)
        for n, ab in enumerate(GRAMS)
    }
    factor = {}
    for a in range(NPOLY):
        for b in range(a + 1):
            value = gram[a, b]
            for m in range(b):
                value = value - factor[a, m] * factor[b, m]
            factor[a, b] = jnp.sqrt(value) if a == b else value / factor[b, b]

    def solve():
        wait_all(rsum.at[pl.ds(1, ndev - 1)], c_send.at[2], c_recv.at[0]).wait_recv()
        rsum[0] = tile_value(rhs, ident)
        part = jnp.sum(rsum[...], axis=0)
        for c in range(2):
            forward = []
            for a in range(NPOLY):
                running = part[c * NPOLY + a : c * NPOLY + a + 1]
                for b in range(a):
                    running = running - factor[a, b] * forward[b]
                forward.append(running / factor[a, a])
            backward = [None] * NPOLY
            for a in reversed(range(NPOLY)):
                running = forward[a]
                for b in range(a + 1, NPOLY):
                    running = running - factor[b, a] * backward[b]
                backward[a] = running / factor[a, a]
            for j in range(NPOLY):
                solved[c * NPOLY + j : c * NPOLY + j + 1] = backward[j]
        for at in range(2 * NPOLY, 8):
            solved[at : at + 1] = jnp.zeros((1, 128), f32)
        coef[
            pl.ds(pl.multiple_of((ident // lanes) * 8, 8), 8),
            pl.ds(pl.multiple_of((ident % lanes) * 128, 128), 128),
        ] = solved[...]
        for o in range(1, ndev):
            remote(
                solved, tile(coef, ident), c_send.at[1], c_recv.at[1], any_peer(o)
            ).start()

    owning(ident, solve)

    for o in range(1, nb):
        residual(o)

    for g in range(nb):
        own = slice(g * fl, (g + 1) * fl)
        for c in range(2):
            for t in range(slots):
                put = (c * slots + t) * fl
                resid_out[c, t, own] = resbuf[g, put : put + fl]
            for k in range(dirn):
                put = c * rows + k * fl
                gains_out[c, k, own] = gall[g, put : put + fl]

    def wait_tiles(count, send, recv, what):
        waiter = wait_all(rsum.at[pl.ds(0, count)], send, recv)
        if what == "send":
            waiter.wait_send()
        else:
            waiter.wait_recv()

    if ndev <= chunks:
        wait_tiles(ndev - 1, c_send.at[1], c_recv.at[1], "recv")
    else:
        @pl.when(ident < chunks)
        def _():
            wait_tiles(chunks - 1, c_send.at[1], c_recv.at[1], "recv")

        @pl.when(ident >= chunks)
        def _():
            wait_tiles(chunks, c_send.at[1], c_recv.at[1], "recv")

    chan = lax.broadcasted_iota(i32, (chans, 128), 0)
    chan_basis = [
        jnp.broadcast_to(b[:, :1], (chans, stations))
        for b in legendre(by(chan, chans, lambda f: ratio[0, f]))
    ]
    for c in range(2):
        for k in range(dirn):
            value = dual[c, k] + gains_out[c, k]
            for j in range(NPOLY):
                put = k * 8 + c * NPOLY + j
                coefficient = coef[put : put + 1]
                cons_out[c, j, k : k + 1] = coefficient
                value = value - chan_basis[j] * coefficient
            dual_out[c, k] = value

    if ndev <= chunks:
        wait_tiles(ndev - 1, c_send.at[0], c_recv.at[0], "send")
        wait_tiles(ndev - 1, c_send.at[1], c_recv.at[1], "send")
    else:
        @pl.when(ident < chunks)
        def _():
            wait_tiles(chunks - 1, c_send.at[0], c_recv.at[0], "send")
            wait_tiles(ndev - 1, c_send.at[1], c_recv.at[1], "send")

        @pl.when(ident >= chunks)
        def _():
            wait_tiles(chunks, c_send.at[0], c_recv.at[0], "send")

    for copy in firsts + seconds + spread:
        copy.wait_send()


def body(nb, nf, vis, flag, pair, coords, dirs, flux, ratio, gains, dual, cons, penalty):
    _, slots, chans, base = vis.shape
    dirn, stations = gains.shape[1], gains.shape[3]
    fl = chans // nb
    rows = dirn * fl
    total = base * nb
    ndev = nb * nf
    ch = min(1024, base)
    half = 128 * (-(-3 * rows // 128))
    rho_scale = 2.0 * total * slots / stations
    sizes = (nb, nf, slots, chans, base, dirn, stations, rho_scale)
    vmem = pl.BlockSpec(memory_space=pltpu.VMEM)
    smem = pl.BlockSpec(memory_space=pltpu.SMEM)
    dma = pltpu.SemaphoreType.DMA
    shape = jax.ShapeDtypeStruct
    return pl.pallas_call(
        functools.partial(kernel, sizes),
        name="admm_step",
        out_shape=(
            shape(gains.shape, f32),
            shape(cons.shape, f32),
            shape(dual.shape, f32),
            shape(vis.shape, f32),
        ),
        in_specs=[vmem, vmem, vmem, vmem, smem, smem, smem, vmem, vmem, vmem, smem],
        out_specs=(vmem, vmem, vmem, vmem),
        scratch_shapes=[
            pltpu.VMEM((stations, 2 * total), bf16),
            pltpu.VMEM((nb, 2 + 2 * slots, base), f32),
            pltpu.VMEM((nb, 3 * slots * fl, base), f32),
            pltpu.VMEM((nb, 3 * slots * fl, base), f32),
            pltpu.VMEM((2, slots, rows, total), f32),
            pltpu.VMEM((nb, 2, slots, rows, base), f32),
            pltpu.VMEM((4, rows, 128), f32),
            pltpu.VMEM((nb, 2, rows, 128), f32),
            pltpu.VMEM((2 * rows, stations), f32),
            pltpu.VMEM((2, 2 * rows, total), f32),
            pltpu.VMEM((1, 4 * rows, stations), bf16),
            pltpu.VMEM((2 * rows, stations), f32),
            pltpu.VMEM((2, slots, 8, total), f32),
            pltpu.VMEM((slots, 8, total), f32),
            pltpu.VMEM((2, slots, 8, total), f32),
            pltpu.VMEM((2 * half, 2 * ch), bf16),
            pltpu.VMEM((stations, 2 * half), f32),
            pltpu.VMEM((nb, 2 * rows, stations), f32),
            pltpu.VMEM((nb, 2 * slots * fl, base), f32),
            pltpu.VMEM((ITERS, ndev, 4, 128), f32),
            pltpu.VMEM((8 * dirn, stations), f32),
            pltpu.VMEM((ndev, 8, 128), f32),
            pltpu.VMEM((8, 128), f32),
            pltpu.VMEM((8 * dirn, stations), f32),
            dma((nb,)),
            dma((nb,)),
            dma((nb,)),
            dma((nb,)),
            dma((ITERS,)),
            dma((ITERS,)),
            dma((nb,)),
            dma((nb,)),
            dma((3,)),
            dma((3,)),
        ],
        compiler_params=pltpu.CompilerParams(
            collective_id=0, has_side_effects=True, vmem_limit_bytes=60 * 1024 * 1024
        ),
    )(vis, flag, pair, coords, dirs, flux, ratio.reshape(1, -1), gains, dual, cons, penalty)


def solution(mesh):
    in_specs = (
        P(None, None, "freq", "bl"),
        P(None, "freq", "bl"),
        P(None, "bl"),
        P(None, None, "bl"),
        P(),
        P(None, "freq"),
        P("freq"),
        P(None, None, "freq", None),
        P(None, None, "freq", None),
        P(),
        P(),
    )
    out_specs = (
        P(None, None, "freq", None),
        P(),
        P(None, None, "freq", None),
        P(None, None, "freq", "bl"),
    )
    step = functools.partial(body, mesh.shape["bl"], mesh.shape["freq"])
    return jax.shard_map(step, mesh=mesh, in_specs=in_specs, out_specs=out_specs, check_vma=False)
```

```python
import functools
import math

import jax
import jax.numpy as jnp
from jax import lax
from jax.experimental import pallas as pl
from jax.experimental.pallas import tpu as pltpu
from jax.sharding import PartitionSpec as P

NPOLY = 3
ITERS = 3

robust_dof = 2.0
small_term = 1e-06
two_pi = 2.0 * math.pi
MESH = pl.DeviceIdType.MESH
TWICE_BYTES = 36 * 1024 * 1024
f32, bf16, i32 = jnp.float32, jnp.bfloat16, jnp.int32

SIN_TERMS = [(-1.0) ** n * two_pi ** (2 * n + 1) / math.factorial(2 * n + 1) for n in range(6)]
COS_TERMS = [(-1.0) ** n * two_pi ** (2 * n) / math.factorial(2 * n) for n in range(7)]
GRAMS = [(a, b) for a in range(NPOLY) for b in range(a + 1)]


def horner(terms, square):
    value = jnp.full_like(square, terms[-1])
    for term in terms[-2::-1]:
        value = value * square + term
    return value


def turn_parts(turns):
    half = jnp.floor(turns * 2.0 + 0.5)
    rest = turns - half * 0.5
    sign = 1.0 - 2.0 * (half - 2.0 * jnp.floor(half * 0.5))
    square = rest * rest
    return horner(COS_TERMS, square), rest * horner(SIN_TERMS, square), sign


def split_two(value):
    high = value.astype(bf16)
    low = (value - high.astype(f32)).astype(bf16)
    return high, low


def legendre(ratio):
    scaled = (ratio - 1.05) / 0.35
    return [jnp.ones_like(scaled), scaled, (3.0 * scaled * scaled - 1.0) / 2.0]


def chunk_of(stations, total, base):
    return min(2048 if fits_twice(stations, total) else 512, base)


def blocks(length, count, body, carry):
    count = math.gcd(length // 128, count)

    def step(i, carry):
        for n in range(count):
            carry = body(i * count + n, carry)
        return carry

    return lax.fori_loop(0, length // 128 // count, step, carry)


def fits_twice(stations, total):
    return 8 * stations * total <= TWICE_BYTES


def kernel(
    sizes,
    vis,
    flag,
    pair,
    coords,
    dirs,
    flux,
    ratio,
    gains_in,
    dual,
    cons_in,
    penalty,
    pack,
    table,
    twin,
    meta,
    sendx,
    xin,
    sky,
    sky_own,
    const,
    const_own,
    anchor,
    side_even,
    side_odd,
    gsplit,
    gcur,
    visd,
    flagd,
    err,
    stack_even,
    stack_odd,
    acc,
    gall,
    resbuf,
    sbuf,
    rhs,
    rsum,
    solved,
    coef,
    weights,
    dual_own,
    m_send,
    m_recv,
    x_send,
    x_recv,
    s_send,
    s_recv,
    g_send,
    g_recv,
    c_send,
    c_recv,
):
    nb, nf, slots, chans, base, dirn, stations, rho_scale = sizes
    fl = chans // nb
    rows = dirn * fl
    units = rows // 16
    total = base * nb
    kp = 8 // fl
    ndev = nb * nf
    paired = fits_twice(stations, total)
    half = 3 * rows if paired else 128 * (-(-3 * rows // 128))
    lanes = stations // 128
    chunks = dirn * lanes
    ch = chunk_of(stations, total, base)
    me = lax.axis_index("bl")
    mf = lax.axis_index("freq")
    ident = me * nf + mf

    def bl_peer(o):
        return lax.bitwise_xor(me, o)

    def any_peer(o):
        return {"bl": lax.bitwise_xor(me, o // nf), "freq": lax.bitwise_xor(mf, o % nf)}

    def remote(src, dst, send, recv, device):
        return pltpu.make_async_remote_copy(
            src_ref=src, dst_ref=dst, send_sem=send, recv_sem=recv,
            device_id=device, device_id_type=MESH,
        )

    barrier = pltpu.get_barrier_semaphore()
    for o in reversed(range(1, ndev)):
        pl.semaphore_signal(barrier, inc=1, device_id=any_peer(o), device_id_type=MESH)

    meta[me, 0:2] = pair[...].astype(f32)
    for c in range(2):
        for t in range(slots):
            meta[me, 2 + c * slots + t : 3 + c * slots + t] = coords[c, t : t + 1]
    for g in range(nb):
        own = slice(g * fl, (g + 1) * fl)
        for t in range(slots):
            for c in range(2):
                at = (c * slots + t) * fl
                sendx[g, at : at + fl] = vis[c, t, own]
            at = (2 * slots + t) * fl
            sendx[g, at : at + fl] = flag[t, own].astype(f32)

    pl.semaphore_wait(barrier, ndev - 1)
    firsts = [
        remote(meta.at[me], meta.at[me], m_send.at[o], m_recv.at[o], {"bl": bl_peer(o)})
        for o in range(1, nb)
    ]
    seconds = [
        remote(sendx.at[bl_peer(o)], xin.at[me], x_send.at[o], x_recv.at[o], {"bl": bl_peer(o)})
        for o in range(1, nb)
    ]
    for copy in firsts[::-1] + seconds[::-1]:
        copy.start()
    xin[me] = sendx[me]

    row = lax.broadcasted_iota(i32, (rows, 128), 0)
    row_k, row_f = row // fl, row % fl

    def by(index, count, pick):
        value = jnp.full(index.shape, pick(0), f32)
        for n in range(1, count):
            value = jnp.where(index == n, pick(n), value)
        return value

    const[0] = by(row_k, dirn, lambda k: dirs[0, k])
    const[1] = by(row_k, dirn, lambda k: dirs[1, k])
    const[2] = by(row_k, dirn, lambda k: penalty[k]) * rho_scale
    for g in range(nb):
        const_own[g, 0] = by(row_f, fl, lambda f: ratio[0, g * fl + f])
        const_own[g, 1] = by(row, rows, lambda r: flux[r // fl, g * fl + r % fl])
    const[3] = const_own[me, 1] * const_own[me, 1]

    def build_table(g):
        iota = lax.broadcasted_iota(i32, (16, 256), 0).astype(jnp.int16)
        one, zero = jnp.ones((16, 256), bf16), jnp.zeros((16, 256), bf16)

        def step(i, carry):
            at = pl.multiple_of(i * 256, 256)
            for s in range(2):
                spot = jnp.broadcast_to(meta[g, s : s + 1, pl.ds(at, 256)].astype(i32), (16, 256))
                spot = spot.astype(jnp.int16)
                where = pl.ds(pl.multiple_of(s * total + g * base + at, 256), 256)
                for r in range(0, stations, 16):
                    table[r : r + 16, where] = jnp.where(spot == iota + jnp.int16(r), one, zero)
            return carry

        lax.fori_loop(0, base // 256, step, 0)

    def build_twin(first, stop):
        iota = lax.broadcasted_iota(i32, (128, 128), 1).astype(jnp.int16)
        one, zero = jnp.ones((128, 128), bf16), jnp.zeros((128, 128), bf16)
        rest = jnp.zeros((6, 128), f32)

        def outer(o, carry):
            g = bl_peer(o)

            def step(i, carry):
                here = pl.ds(pl.multiple_of(i * 128, 128), 128)
                turned = jnp.concatenate([meta[g, 0:2, here], rest], axis=0).T
                at = g * base + i * 128
                for s in range(2):
                    put = at // ch * (2 * ch) + s * ch + at % ch
                    spot = jnp.broadcast_to(turned[:, s : s + 1], (128, 128))
                    spot = spot.astype(i32).astype(jnp.int16)
                    for l in range(lanes):
                        hit = spot == iota + jnp.int16(128 * l)
                        twin[
                            pl.ds(pl.multiple_of(put, 128), 128), l * 128 : (l + 1) * 128
                        ] = jnp.where(hit, one, zero)
                return carry

            return blocks(base, 8, step, carry)

        lax.fori_loop(first, stop, outer, 0)

    def build_sky(g, coord, put):
        def step(i, carry):
            cols = pl.ds(pl.multiple_of(i * 128, 128), 128)
            for t in range(slots):
                u, v = coord(t, cols)
                for w in range(units):
                    at = slice(w * 16, (w + 1) * 16)
                    project = const[0, at] * u + const[1, at] * v
                    cosine, sine, sign = turn_parts(project * const_own[g, 0, at])
                    amplitude = sign * const_own[g, 1, at]
                    put(t, at, i, amplitude * cosine, amplitude * sine)
            return carry

        blocks(base, 2, step, 0)

    def setup(g):
        build_table(g)

        def coord(t, cols):
            return meta[g, 2 + t : 3 + t, cols], meta[g, 2 + slots + t : 3 + slots + t, cols]

        def put(t, at, i, re, im):
            cols = pl.ds(pl.multiple_of(g * base + i * 128, 128), 128)
            sky[0, t, at, cols] = re
            sky[1, t, at, cols] = im

        build_sky(me, coord, put)

    setup(me)

    lane = lax.broadcasted_iota(i32, (1, 128), 1)
    gram_row = jnp.zeros((1, 128), f32)
    for n, (a, b) in enumerate(GRAMS):
        entry = jnp.zeros((1, 128), f32)
        for f in range(fl):
            basis = legendre(jnp.full((1, 128), ratio[0, me * fl + f], f32))
            entry = entry + basis[a] * basis[b]
        gram_row = gram_row + jnp.where(lane == n, entry, 0.0)
    for it in range(ITERS):
        sbuf[it, 0, 2:3] = gram_row
        sbuf[it, 0, 3:4] = jnp.zeros((1, 128), f32)

    def wide(column):
        return jnp.broadcast_to(column[:, :1], (rows, stations))

    def own_rows(ref, c, k):
        value = ref[c, k, 0:fl]
        for g in range(1, nb):
            value = jnp.where(me == g, ref[c, k, g * fl : (g + 1) * fl], value)
        return value

    basis_rows = legendre(const_own[me, 0])
    for c in range(2):
        for k in range(dirn):
            at = k * fl
            gcur[c * rows + at : c * rows + at + fl] = own_rows(gains_in, c, k)
            value = -own_rows(dual, c, k)
            for j in range(NPOLY):
                weight = basis_rows[j][at : at + fl, :1]
                value = value + weight * cons_in[c, j, k : k + 1]
            anchor[c * rows + at : c * rows + at + fl] = value * const[2, at : at + fl, :1]
    stack_even[...] = jnp.zeros_like(stack_even)
    stack_odd[...] = jnp.zeros_like(stack_odd)

    def put_split(slot, value):
        high, low = split_two(value)
        gsplit[slot, 0 : 2 * rows] = high
        gsplit[slot, 2 * rows : 4 * rows] = low

    put_split(0, gcur[...])
    for o in range(1, nb):
        firsts[o - 1].wait_recv()
        setup(bl_peer(o))

    def gather(slot, off, width):
        both = jnp.dot(
            gsplit[slot], table[:, pl.ds(off, width)], preferred_element_type=f32
        )
        return both[: 2 * rows] + both[2 * rows :]

    def fold(value):
        value = value[:8] + value[8:]
        shift = fl
        while shift < 8:
            value = value + pltpu.roll(value, shift, 0)
            shift *= 2
        return value

    def model(left, right, sub, field, cols):
        inside = slice(sub * 128, (sub + 1) * 128)
        real, imag = [None] * slots, [None] * slots
        for w in range(units):
            re, im = slice(w * 16, w * 16 + 16), slice(rows + w * 16, rows + w * 16 + 16)
            lr, li = left[re, inside], left[im, inside]
            rr, ri = right[re, inside], right[im, inside]
            pr = lr * rr + li * ri
            pi = li * rr - lr * ri
            for t in range(slots):
                sr, si = field(0, t, re, cols), field(1, t, re, cols)
                mr, mi = pr * sr - pi * si, pr * si + pi * sr
                real[t] = mr if w == 0 else real[t] + mr
                imag[t] = mi if w == 0 else imag[t] + mi
        return [fold(v) for v in real], [fold(v) for v in imag]

    def sky_all(c, t, at, cols):
        return sky[c, t, at, cols]

    def gather_pair(side, i, odd):
        at = pl.multiple_of((2 * i + odd) * ch, ch)
        here = pl.ds(pl.multiple_of(i * ch, ch), ch)
        side[0, :, here] = gather(0, at, ch)
        side[1, :, here] = gather(0, pl.multiple_of(total + at, ch), ch)

    def predict(observed):
        def elements(side, i, odd, misfit):
            at = (2 * i + odd) * ch
            here = pl.ds(pl.multiple_of(i * ch, ch), ch)
            left, right = side.at[0, :, here], side.at[1, :, here]
            for sub in range(ch // 128):
                cols = pl.ds(pl.multiple_of(at + sub * 128, 128), 128)
                real, imag = model(left, right, sub, sky_all, cols)
                for t in range(slots):
                    if observed:
                        real[t] = visd[0, t, :, cols] - real[t]
                        imag[t] = visd[1, t, :, cols] - imag[t]
                        power = real[t] * real[t] + imag[t] * imag[t]
                        misfit = misfit + flagd[t, :, cols] * power
                    err[0, t, :, cols] = real[t]
                    err[1, t, :, cols] = imag[t]
            return misfit

        def step(i, misfit):
            gather_pair(side_odd, i, 1)
            misfit = elements(side_even, i, 0, misfit)
            gather_pair(side_even, i + 1, 0)
            return elements(side_odd, i, 1, misfit)

        last = total // ch // 2 - 1
        gather_pair(side_even, 0, 0)
        misfit = lax.fori_loop(0, last, step, jnp.zeros((8, 128), f32))
        gather_pair(side_odd, last, 1)
        misfit = elements(side_even, last, 0, misfit)
        return elements(side_odd, last, 1, misfit)

    def put_sum(it, at, value):
        sbuf[it, 0, at : at + 1] = jnp.sum(value, axis=0, keepdims=True) * (1.0 / kp)

    predict(False)
    if paired:
        build_twin(0, nb // 2)
    for copy in seconds:
        copy.wait_recv()

    def spread_rows(value):
        return jnp.concatenate([value] * kp, axis=0)

    def observe():
        def outer(g, sums):
            def step(i, sums):
                misfit, count = sums
                here = pl.ds(pl.multiple_of(i * 128, 128), 128)
                cols = pl.ds(pl.multiple_of(g * base + i * 128, 128), 128)
                for t in range(slots):
                    at = (2 * slots + t) * fl
                    weight = spread_rows(xin[g, at : at + fl, here])
                    flagd[t, :, cols] = weight
                    count = count + weight
                    power = None
                    for c in range(2):
                        at = (c * slots + t) * fl
                        seen = spread_rows(xin[g, at : at + fl, here])
                        visd[c, t, :, cols] = seen
                        value = seen - err[c, t, :, cols]
                        err[c, t, :, cols] = value
                        power = value * value if c == 0 else power + value * value
                    misfit = misfit + weight * power
                return misfit, count

            return blocks(base, 4, step, sums)

        zero = jnp.zeros((8, 128), f32)
        return lax.fori_loop(0, nb, outer, (zero, zero))

    def wait_all(ref, send, recv):
        return remote(ref, ref, send, recv, any_peer(1))

    def build_own_sky():
        for g in range(nb):
            def coord(t, cols):
                return coords[0, t : t + 1, cols], coords[1, t : t + 1, cols]

            def put(t, at, i, re, im, g=g):
                cols = pl.ds(pl.multiple_of(i * 128, 128), 128)
                sky_own[g, 0, t, at, cols] = re
                sky_own[g, 1, t, at, cols] = im

            build_sky(g, coord, put)

    def prepare_end():
        lanes_of = lax.broadcasted_iota(i32, (8 * dirn, 2 * rows), 1)
        rows_of = lax.broadcasted_iota(i32, (8 * dirn, 2 * rows), 0)
        ratio_lanes = by(lanes_of % fl, fl, lambda f: ratio[0, me * fl + f])
        basis = legendre(ratio_lanes)
        place = rows_of % 8
        value = jnp.zeros((8 * dirn, 2 * rows), f32)
        for c in range(2):
            for j in range(NPOLY):
                hit = (place == c * NPOLY + j) & (lanes_of // rows == c)
                hit = hit & ((lanes_of % rows) // fl == rows_of // 8)
                value = jnp.where(hit, basis[j], value)
        weights[...] = value
        chan = lax.broadcasted_iota(i32, (chans, 128), 0)
        basis = legendre(by(chan, chans, lambda f: ratio[0, f]))
        for j in range(NPOLY):
            pack[pack.shape[0] - 1, :, j * 128 : (j + 1) * 128] = basis[j]
        for c in range(2):
            for k in range(dirn):
                put = c * rows + k * fl
                dual_own[put : put + fl] = own_rows(dual, c, k)

    def iteration(it, carry):
        @pl.when(it == 0)
        def _():
            misfit, count = observe()
            for n in range(ITERS):
                put_sum(n, 1, count)
            put_sum(it, 0, misfit)

        @pl.when(it > 0)
        def _():
            put_sum(it, 0, predict(True))

        for o in reversed(range(1, ndev)):
            remote(
                sbuf.at[it, 0], sbuf.at[it, o], s_send.at[it], s_recv.at[it], any_peer(o)
            ).start()

        if paired:
            pl.when(it == 0)(lambda: build_twin(nb // 2, nb))
        pl.when(it == 1)(build_own_sky)
        pl.when(it == 2)(prepare_end)

        finish = wait_all(sbuf.at[it, pl.ds(1, ndev - 1)], s_send.at[it], s_recv.at[it])
        finish.wait_recv()
        sums = jnp.sum(sbuf[it], axis=0)
        sums = jnp.sum(sums, axis=1, keepdims=True)
        sigma_sq = sums[0:1] / (sums[1:2] + 1.0) + small_term
        inverse = 1.0 / sigma_sq
        acc[...] = jnp.zeros_like(acc)

        def normal(side, stacked, i, odd):
            at = (2 * i + odd) * ch
            for sub in range(ch // 128):
                cols = pl.ds(pl.multiple_of(at + sub * 128, 128), 128)
                here = pl.ds(pl.multiple_of(i * ch + sub * 128, 128), 128)
                weighted, wsum = [], None
                for t in range(slots):
                    er, ei = err[0, t, :, cols], err[1, t, :, cols]
                    power = er * er + ei * ei
                    r = flagd[t, :, cols] * (robust_dof + 1.0) / (robust_dof + power * inverse)
                    weighted.append([jnp.concatenate([r * e, r * e], axis=0) for e in (er, ei)])
                    wsum = r if t == 0 else wsum + r
                wsum = jnp.concatenate([wsum, wsum], axis=0)
                for w in range(units):
                    re, im = slice(w * 16, w * 16 + 16), slice(rows + w * 16, rows + w * 16 + 16)
                    lr, li = side[0, re, here], side[0, im, here]
                    rr, ri = side[1, re, here], side[1, im, here]
                    c2 = const[3, re] * wsum
                    xr = (lr * rr + li * ri) * c2
                    xi = (li * rr - lr * ri) * c2
                    for t in range(slots):
                        sr, si = sky[0, t, re, cols], sky[1, t, re, cols]
                        wr, wi = weighted[t]
                        xr = xr + (sr * wr + si * wi)
                        xi = xi + (sr * wi - si * wr)
                    terms = (
                        (rr * xr - ri * xi, lr * xr + li * xi),
                        (rr * xi + ri * xr, li * xr - lr * xi),
                        ((rr * rr + ri * ri) * c2, (lr * lr + li * li) * c2),
                    )
                    for q in range(3):
                        for s in range(2):
                            high, low = split_two(terms[q][s])
                            put = q * rows + w * 16
                            where = slice(s * ch + sub * 128, s * ch + sub * 128 + 128)
                            stacked[put : put + 16, where] = high
                            stacked[half + put : half + put + 16, where] = low

        def add_up(stacked, i, odd):
            at = (2 * i + odd) * ch
            if paired:
                acc[...] += jnp.dot(
                    stacked[...],
                    twin[pl.ds(pl.multiple_of(2 * at, 2 * ch), 2 * ch), :],
                    preferred_element_type=f32,
                )
                return
            for s in range(2):
                acc[...] += lax.dot_general(
                    table[:, pl.ds(pl.multiple_of(s * total + at, ch), ch)],
                    stacked[:, s * ch : (s + 1) * ch],
                    (((1,), (1,)), ((), ())),
                    preferred_element_type=f32,
                )

        def normal_pair(i, carry):
            add_up(stack_even, i, 0)
            normal(side_odd, stack_odd, i, 1)
            add_up(stack_odd, i, 1)
            normal(side_even, stack_even, i + 1, 0)
            return carry

        last = total // ch // 2 - 1
        normal(side_even, stack_even, 0, 0)
        lax.fori_loop(0, last, normal_pair, 0)
        add_up(stack_even, last, 0)
        normal(side_odd, stack_odd, last, 1)
        add_up(stack_odd, last, 1)
        if paired:
            normals = acc[:half] + acc[half:]
        else:
            normals = (acc[:, :half] + acc[:, half:]).T
        divisor = 1.0 / (normals[2 * rows : 3 * rows] + wide(const[2]))
        for c in range(2):
            at = slice(c * rows, (c + 1) * rows)
            gcur[at] = 0.5 * (gcur[at] + (normals[at] + anchor[at]) * divisor)
        put_split(0, gcur[...])
        finish.wait_send()
        return carry

    lax.fori_loop(0, ITERS, iteration, 0)

    both = gcur[...] + dual_own[...]
    rhs[...] = jnp.dot(
        weights[...], both, preferred_element_type=f32, precision=lax.Precision.HIGHEST
    )

    def tile(ref, n):
        return ref.at[
            pl.ds(pl.multiple_of((n // lanes) * 8, 8), 8),
            pl.ds(pl.multiple_of((n % lanes) * 128, 128), 128),
        ]

    def tile_value(ref, n):
        return ref[
            pl.ds(pl.multiple_of((n // lanes) * 8, 8), 8),
            pl.ds(pl.multiple_of((n % lanes) * 128, 128), 128),
        ]

    def owning(n, action):
        if ndev <= chunks:
            action()
        else:
            pl.when(n < chunks)(action)

    def ident_of(o):
        peer = any_peer(o)
        return peer["bl"] * nf + peer["freq"]

    for o in reversed(range(1, ndev)):
        n = ident_of(o)

        def send(o=o, n=n):
            remote(
                tile(rhs, n), rsum.at[o], c_send.at[0], c_recv.at[0], any_peer(o)
            ).start()

        owning(n, send)

    gall[me] = gcur[...]
    spread = [
        remote(gall.at[me], gall.at[me], g_send.at[o], g_recv.at[o], {"bl": bl_peer(o)})
        for o in range(1, nb)
    ]
    for copy in spread:
        copy.start()

    def residual(o):
        g = bl_peer(o)
        if o > 0:
            spread[o - 1].wait_recv()
            put_split(0, gall[g])

        def sky_here(c, t, at, cols):
            return sky_own[g, c, t, at, cols]

        sides = []
        for at in range(0, base, ch):
            off = me * base + at
            sides.append(
                (gather(0, pl.multiple_of(off, ch), ch), gather(0, pl.multiple_of(total + off, ch), ch))
            )
        for n, (left, right) in enumerate(sides):
            for sub in range(ch // 128):
                cols = pl.ds(n * ch + sub * 128, 128)
                parts = model(left, right, sub, sky_here, cols)
                for c in range(2):
                    for t in range(slots):
                        put = (c * slots + t) * fl
                        resbuf[g, put : put + fl, cols] = (
                            sendx[g, put : put + fl, cols] - parts[c][t][:fl]
                        )

    residual(0)

    gram_total = jnp.sum(sbuf[0, :, 2:3], axis=0)
    gram = {
        ab: jnp.sum(jnp.where(lane == n, gram_total, 0.0), axis=1, keepdims=True)
        for n, ab in enumerate(GRAMS)
    }
    factor = {}
    for a in range(NPOLY):
        for b in range(a + 1):
            value = gram[a, b]
            for m in range(b):
                value = value - factor[a, m] * factor[b, m]
            factor[a, b] = jnp.sqrt(value) if a == b else value / factor[b, b]

    def solve():
        wait_all(rsum.at[pl.ds(1, ndev - 1)], c_send.at[2], c_recv.at[0]).wait_recv()
        rsum[0] = tile_value(rhs, ident)
        part = jnp.sum(rsum[...], axis=0)
        for c in range(2):
            forward = []
            for a in range(NPOLY):
                running = part[c * NPOLY + a : c * NPOLY + a + 1]
                for b in range(a):
                    running = running - factor[a, b] * forward[b]
                forward.append(running / factor[a, a])
            backward = [None] * NPOLY
            for a in reversed(range(NPOLY)):
                running = forward[a]
                for b in range(a + 1, NPOLY):
                    running = running - factor[b, a] * backward[b]
                backward[a] = running / factor[a, a]
            for j in range(NPOLY):
                solved[c * NPOLY + j : c * NPOLY + j + 1] = backward[j]
        for at in range(2 * NPOLY, 8):
            solved[at : at + 1] = jnp.zeros((1, 128), f32)
        coef[
            pl.ds(pl.multiple_of((ident // lanes) * 8, 8), 8),
            pl.ds(pl.multiple_of((ident % lanes) * 128, 128), 128),
        ] = solved[...]
        for o in reversed(range(1, ndev)):
            remote(
                solved, tile(coef, ident), c_send.at[1], c_recv.at[1], any_peer(o)
            ).start()

    owning(ident, solve)

    for o in range(1, nb):
        residual(o)

    for g in range(nb):
        own = slice(g * fl, (g + 1) * fl)
        for c in range(2):
            for t in range(slots):
                put = (c * slots + t) * fl
                for q in range(base // stations):
                    spot = 2 * dirn + (c * slots + t) * (base // stations) + q
                    pack[spot, own] = resbuf[g, put : put + fl, q * stations : (q + 1) * stations]
            for k in range(dirn):
                put = c * rows + k * fl
                pack[c * dirn + k, own] = gall[g, put : put + fl]

    def wait_tiles(count, send, recv, what):
        waiter = wait_all(rsum.at[pl.ds(0, count)], send, recv)
        if what == "send":
            waiter.wait_send()
        else:
            waiter.wait_recv()

    if ndev <= chunks:
        wait_tiles(ndev - 1, c_send.at[1], c_recv.at[1], "recv")
    else:
        @pl.when(ident < chunks)
        def _():
            wait_tiles(chunks - 1, c_send.at[1], c_recv.at[1], "recv")

        @pl.when(ident >= chunks)
        def _():
            wait_tiles(chunks, c_send.at[1], c_recv.at[1], "recv")

    spot = 2 * dirn + 2 * slots * (base // stations)
    for n in range(8 * dirn // chans):
        pack[spot + n] = coef[n * chans : (n + 1) * chans]

    if ndev <= chunks:
        wait_tiles(ndev - 1, c_send.at[0], c_recv.at[0], "send")
        wait_tiles(ndev - 1, c_send.at[1], c_recv.at[1], "send")
    else:
        @pl.when(ident < chunks)
        def _():
            wait_tiles(chunks - 1, c_send.at[0], c_recv.at[0], "send")
            wait_tiles(ndev - 1, c_send.at[1], c_recv.at[1], "send")

        @pl.when(ident >= chunks)
        def _():
            wait_tiles(chunks, c_send.at[0], c_recv.at[0], "send")

    for copy in firsts + seconds + spread:
        copy.wait_send()


def finish_kernel(sizes, pack, dual, gains_out, cons_out, dual_out, resid_out, cons, new_dual, sems):
    slots, chans, base, dirn, stations = sizes
    wide = base // stations
    copies = []

    def send(src, dst):
        copies.append(pltpu.make_async_copy(src, dst, sems.at[len(copies)]))
        copies[-1].start()

    for c in range(2):
        for t in range(slots):
            for q in range(wide):
                spot = 2 * dirn + (c * slots + t) * wide + q
                send(pack.at[spot], resid_out.at[c, t, :, pl.ds(q * stations, stations)])
        send(pack.at[pl.ds(c * dirn, dirn)], gains_out.at[c])
    last = pack.shape[0] - 1
    basis = [
        jnp.broadcast_to(pack[last, :, j * 128 : j * 128 + 1], (chans, stations))
        for j in range(NPOLY)
    ]
    spot = 2 * dirn + 2 * slots * wide
    for c in range(2):
        for k in range(dirn):
            value = dual[c, k] + pack[c * dirn + k]
            for j in range(NPOLY):
                put = k * 8 + c * NPOLY + j
                coefficient = pack[spot + put // chans, put % chans : put % chans + 1]
                cons[c, j, k : k + 1] = coefficient
                value = value - basis[j] * coefficient
            new_dual[c, k] = value
        send(new_dual.at[c], dual_out.at[c])
    send(cons, cons_out)
    for copy in copies:
        copy.wait()


def body(nb, nf, vis, flag, pair, coords, dirs, flux, ratio, gains, dual, cons, penalty):
    _, slots, chans, base = vis.shape
    dirn, stations = gains.shape[1], gains.shape[3]
    fl = chans // nb
    rows = dirn * fl
    total = base * nb
    ndev = nb * nf
    ch = chunk_of(stations, total, base)
    paired = fits_twice(stations, total)
    half = 3 * rows if paired else 128 * (-(-3 * rows // 128))
    ratio = ratio.reshape(1, -1)
    rho_scale = 2.0 * total * slots / stations
    sizes = (nb, nf, slots, chans, base, dirn, stations, rho_scale)
    vmem = pl.BlockSpec(memory_space=pltpu.VMEM)
    smem = pl.BlockSpec(memory_space=pltpu.SMEM)
    dma = pltpu.SemaphoreType.DMA
    shape = jax.ShapeDtypeStruct
    wide = base // stations
    blocks_out = 2 * dirn + 2 * slots * wide + 8 * dirn // chans + 1
    (pack,) = pl.pallas_call(
        functools.partial(kernel, sizes),
        name="admm_step",
        out_shape=(
            shape((blocks_out, chans, stations), f32),
        ),
        in_specs=[vmem, vmem, vmem, vmem, smem, smem, smem, vmem, vmem, vmem, smem],
        out_specs=(vmem,),
        scratch_shapes=[
            pltpu.VMEM((stations, 2 * total), bf16),
            pltpu.VMEM((2 * total, stations) if paired else (16, 128), bf16),
            pltpu.VMEM((nb, 2 + 2 * slots, base), f32),
            pltpu.VMEM((nb, 3 * slots * fl, base), f32),
            pltpu.VMEM((nb, 3 * slots * fl, base), f32),
            pltpu.VMEM((2, slots, rows, total), f32),
            pltpu.VMEM((nb, 2, slots, rows, base), f32),
            pltpu.VMEM((4, rows, 128), f32),
            pltpu.VMEM((nb, 2, rows, 128), f32),
            pltpu.VMEM((2 * rows, stations), f32),
            pltpu.VMEM((2, 2 * rows, total // 2), f32),
            pltpu.VMEM((2, 2 * rows, total // 2), f32),
            pltpu.VMEM((1, 4 * rows, stations), bf16),
            pltpu.VMEM((2 * rows, stations), f32),
            pltpu.VMEM((2, slots, 8, total), f32),
            pltpu.VMEM((slots, 8, total), f32),
            pltpu.VMEM((2, slots, 8, total), f32),
            pltpu.VMEM((2 * half, 2 * ch), bf16),
            pltpu.VMEM((2 * half, 2 * ch), bf16),
            pltpu.VMEM((2 * half, stations) if paired else (stations, 2 * half), f32),
            pltpu.VMEM((nb, 2 * rows, stations), f32),
            pltpu.VMEM((nb, 2 * slots * fl, base), f32),
            pltpu.VMEM((ITERS, ndev, 4, 128), f32),
            pltpu.VMEM((8 * dirn, stations), f32),
            pltpu.VMEM((ndev, 8, 128), f32),
            pltpu.VMEM((8, 128), f32),
            pltpu.VMEM((8 * dirn, stations), f32),
            pltpu.VMEM((8 * dirn, 2 * rows), f32),
            pltpu.VMEM((2 * rows, stations), f32),
            dma((nb,)),
            dma((nb,)),
            dma((nb,)),
            dma((nb,)),
            dma((ITERS,)),
            dma((ITERS,)),
            dma((nb,)),
            dma((nb,)),
            dma((3,)),
            dma((3,)),
        ],
        compiler_params=pltpu.CompilerParams(
            collective_id=0, has_side_effects=True, vmem_limit_bytes=60 * 1024 * 1024
        ),
    )(vis, flag, pair, coords, dirs, flux, ratio, gains, dual, cons, penalty)
    anywhere = pl.BlockSpec(memory_space=pl.ANY)
    return pl.pallas_call(
        functools.partial(finish_kernel, (slots, chans, base, dirn, stations)),
        name="finish",
        out_shape=(
            shape(gains.shape, f32),
            shape(cons.shape, f32),
            shape(dual.shape, f32),
            shape(vis.shape, f32),
        ),
        in_specs=[vmem, vmem],
        out_specs=(anywhere, anywhere, anywhere, anywhere),
        scratch_shapes=[
            pltpu.VMEM(cons.shape, f32),
            pltpu.VMEM(dual.shape, f32),
            dma((2 * slots * wide + 5,)),
        ],
        compiler_params=pltpu.CompilerParams(vmem_limit_bytes=16 * 1024 * 1024),
    )(pack, dual)


def solution(mesh):
    in_specs = (
        P(None, None, "freq", "bl"),
        P(None, "freq", "bl"),
        P(None, "bl"),
        P(None, None, "bl"),
        P(),
        P(None, "freq"),
        P("freq"),
        P(None, None, "freq", None),
        P(None, None, "freq", None),
        P(),
        P(),
    )
    out_specs = (
        P(None, None, "freq", None),
        P(),
        P(None, None, "freq", None),
        P(None, None, "freq", "bl"),
    )
    step = functools.partial(body, mesh.shape["bl"], mesh.shape["freq"])
    return jax.shard_map(step, mesh=mesh, in_specs=in_specs, out_specs=out_specs, check_vma=False)
```

```python
import functools
import math

import jax
import jax.numpy as jnp
from jax import lax
from jax.experimental import pallas as pl
from jax.experimental.pallas import tpu as pltpu
from jax.sharding import PartitionSpec as P

NPOLY = 3
ITERS = 3

robust_dof = 2.0
small_term = 1e-06
two_pi = 2.0 * math.pi
MESH = pl.DeviceIdType.MESH
TWICE_BYTES = 36 * 1024 * 1024
f32, bf16, i32 = jnp.float32, jnp.bfloat16, jnp.int32

SIN_TERMS = [(-1.0) ** n * two_pi ** (2 * n + 1) / math.factorial(2 * n + 1) for n in range(6)]
COS_TERMS = [(-1.0) ** n * two_pi ** (2 * n) / math.factorial(2 * n) for n in range(7)]
GRAMS = [(a, b) for a in range(NPOLY) for b in range(a + 1)]


def horner(terms, square):
    value = jnp.full_like(square, terms[-1])
    for term in terms[-2::-1]:
        value = value * square + term
    return value


def turn_parts(turns):
    half = jnp.floor(turns * 2.0 + 0.5)
    rest = turns - half * 0.5
    sign = 1.0 - 2.0 * (half - 2.0 * jnp.floor(half * 0.5))
    square = rest * rest
    return horner(COS_TERMS, square), rest * horner(SIN_TERMS, square), sign


def split_two(value):
    high = value.astype(bf16)
    low = (value - high.astype(f32)).astype(bf16)
    return high, low


def legendre(ratio):
    scaled = (ratio - 1.05) / 0.35
    return [jnp.ones_like(scaled), scaled, (3.0 * scaled * scaled - 1.0) / 2.0]


def chunk_of(stations, total, base):
    return min(2048 if fits_twice(stations, total) else 512, base)


PART = 512
WIDTH = 512


def part_of(ch):
    return min(PART, ch)


def blocks(length, count, body, carry):
    count = math.gcd(length // 128, count)

    def step(i, carry):
        for n in range(count):
            carry = body(i * count + n, carry)
        return carry

    return lax.fori_loop(0, length // 128 // count, step, carry)


def fits_twice(stations, total):
    return 8 * stations * total <= TWICE_BYTES


def kernel(
    sizes,
    vis,
    flag,
    pair,
    coords,
    dirs,
    flux,
    ratio,
    gains_in,
    dual,
    cons_in,
    penalty,
    pack,
    table,
    twin,
    meta,
    sendx,
    xin,
    sky,
    sky_own,
    const,
    const_own,
    anchor,
    side_even,
    side_odd,
    gsplit,
    gcur,
    visd,
    flagd,
    err,
    stack_even,
    stack_odd,
    acc,
    gall,
    resbuf,
    sbuf,
    fixed,
    rhs,
    rsum,
    solved,
    coef,
    weights,
    dual_own,
    m_send,
    m_recv,
    x_send,
    x_recv,
    s_send,
    s_recv,
    g_send,
    g_recv,
    c_send,
    c_recv,
):
    nb, nf, slots, chans, base, dirn, stations, rho_scale = sizes
    fl = chans // nb
    rows = dirn * fl
    units = rows // 16
    total = base * nb
    kp = 8 // fl
    ndev = nb * nf
    paired = fits_twice(stations, total)
    half = 3 * rows if paired else 128 * (-(-3 * rows // 128))
    lanes = stations // 128
    chunks = dirn * lanes
    ch = chunk_of(stations, total, base)
    part = part_of(ch)
    width = min(WIDTH, ch)
    me = lax.axis_index("bl")
    mf = lax.axis_index("freq")
    ident = me * nf + mf

    def bl_peer(o):
        return lax.bitwise_xor(me, o)

    def any_peer(o):
        return {"bl": lax.bitwise_xor(me, o // nf), "freq": lax.bitwise_xor(mf, o % nf)}

    def remote(src, dst, send, recv, device):
        return pltpu.make_async_remote_copy(
            src_ref=src, dst_ref=dst, send_sem=send, recv_sem=recv,
            device_id=device, device_id_type=MESH,
        )

    barrier = pltpu.get_barrier_semaphore()
    for o in reversed(range(1, ndev)):
        pl.semaphore_signal(barrier, inc=1, device_id=any_peer(o), device_id_type=MESH)

    meta[me, 0:2] = pair[...].astype(f32)
    for c in range(2):
        for t in range(slots):
            meta[me, 2 + c * slots + t : 3 + c * slots + t] = coords[c, t : t + 1]
    for g in range(nb):
        own = slice(g * fl, (g + 1) * fl)
        for t in range(slots):
            for c in range(2):
                at = (c * slots + t) * fl
                sendx[g, at : at + fl] = vis[c, t, own]
            at = (2 * slots + t) * fl
            sendx[g, at : at + fl] = flag[t, own].astype(f32)

    pl.semaphore_wait(barrier, ndev - 1)
    firsts = [
        remote(meta.at[me], meta.at[me], m_send.at[o], m_recv.at[o], {"bl": bl_peer(o)})
        for o in range(1, nb)
    ]
    seconds = [
        remote(sendx.at[bl_peer(o)], xin.at[me], x_send.at[o], x_recv.at[o], {"bl": bl_peer(o)})
        for o in range(1, nb)
    ]
    for copy in firsts[::-1] + seconds[::-1]:
        copy.start()
    xin[me] = sendx[me]

    row = lax.broadcasted_iota(i32, (rows, 128), 0)
    row_k, row_f = row // fl, row % fl

    def by(index, count, pick):
        value = jnp.full(index.shape, pick(0), f32)
        for n in range(1, count):
            value = jnp.where(index == n, pick(n), value)
        return value

    const[0] = by(row_k, dirn, lambda k: dirs[0, k])
    const[1] = by(row_k, dirn, lambda k: dirs[1, k])
    const[2] = by(row_k, dirn, lambda k: penalty[k]) * rho_scale
    for g in range(nb):
        const_own[g, 0] = by(row_f, fl, lambda f: ratio[0, g * fl + f])
        const_own[g, 1] = by(row, rows, lambda r: flux[r // fl, g * fl + r % fl])
    const[3] = const_own[me, 1] * const_own[me, 1]

    def build_table(g):
        iota = lax.broadcasted_iota(i32, (16, 256), 0).astype(jnp.int16)
        one, zero = jnp.ones((16, 256), bf16), jnp.zeros((16, 256), bf16)

        def step(i, carry):
            at = pl.multiple_of(i * 256, 256)
            for s in range(2):
                spot = jnp.broadcast_to(meta[g, s : s + 1, pl.ds(at, 256)].astype(i32), (16, 256))
                spot = spot.astype(jnp.int16)
                where = pl.ds(pl.multiple_of(s * total + g * base + at, 256), 256)
                for r in range(0, stations, 16):
                    table[r : r + 16, where] = jnp.where(spot == iota + jnp.int16(r), one, zero)
            return carry

        lax.fori_loop(0, base // 256, step, 0)

    def build_twin(first, stop):
        iota = lax.broadcasted_iota(i32, (128, 128), 1).astype(jnp.int16)
        one, zero = jnp.ones((128, 128), bf16), jnp.zeros((128, 128), bf16)
        rest = jnp.zeros((6, 128), f32)

        def outer(o, carry):
            g = bl_peer(o)

            def step(i, carry):
                here = pl.ds(pl.multiple_of(i * 128, 128), 128)
                turned = jnp.concatenate([meta[g, 0:2, here], rest], axis=0).T
                at = g * base + i * 128
                for s in range(2):
                    put = at // part * (2 * part) + s * part + at % part
                    spot = jnp.broadcast_to(turned[:, s : s + 1], (128, 128))
                    spot = spot.astype(i32).astype(jnp.int16)
                    for l in range(lanes):
                        hit = spot == iota + jnp.int16(128 * l)
                        twin[
                            pl.ds(pl.multiple_of(put, 128), 128), l * 128 : (l + 1) * 128
                        ] = jnp.where(hit, one, zero)
                return carry

            return blocks(base, 8, step, carry)

        lax.fori_loop(first, stop, outer, 0)

    def build_sky(g, coord, put):
        def step(i, carry):
            cols = pl.ds(pl.multiple_of(i * 128, 128), 128)
            for t in range(slots):
                u, v = coord(t, cols)
                for w in range(units):
                    at = slice(w * 16, (w + 1) * 16)
                    project = const[0, at] * u + const[1, at] * v
                    cosine, sine, sign = turn_parts(project * const_own[g, 0, at])
                    amplitude = sign * const_own[g, 1, at]
                    put(t, at, i, amplitude * cosine, amplitude * sine)
            return carry

        blocks(base, 2, step, 0)

    def setup(g):
        build_table(g)

        def coord(t, cols):
            return meta[g, 2 + t : 3 + t, cols], meta[g, 2 + slots + t : 3 + slots + t, cols]

        def put(t, at, i, re, im):
            cols = pl.ds(pl.multiple_of(g * base + i * 128, 128), 128)
            sky[0, t, at, cols] = re
            sky[1, t, at, cols] = im

        build_sky(me, coord, put)

    setup(me)

    lane = lax.broadcasted_iota(i32, (1, 128), 1)
    gram_row = jnp.zeros((1, 128), f32)
    for n, (a, b) in enumerate(GRAMS):
        entry = jnp.zeros((1, 128), f32)
        for f in range(fl):
            basis = legendre(jnp.full((1, 128), ratio[0, me * fl + f], f32))
            entry = entry + basis[a] * basis[b]
        gram_row = gram_row + jnp.where(lane == 96 + n, entry, 0.0)

    def wide(column):
        return jnp.broadcast_to(column[:, :1], (rows, stations))

    def own_rows(ref, c, k):
        value = ref[c, k, 0:fl]
        for g in range(1, nb):
            value = jnp.where(me == g, ref[c, k, g * fl : (g + 1) * fl], value)
        return value

    basis_rows = legendre(const_own[me, 0])
    for c in range(2):
        for k in range(dirn):
            at = k * fl
            gcur[c * rows + at : c * rows + at + fl] = own_rows(gains_in, c, k)
            value = -own_rows(dual, c, k)
            for j in range(NPOLY):
                weight = basis_rows[j][at : at + fl, :1]
                value = value + weight * cons_in[c, j, k : k + 1]
            anchor[c * rows + at : c * rows + at + fl] = value * const[2, at : at + fl, :1]
    stack_even[...] = jnp.zeros_like(stack_even)
    stack_odd[...] = jnp.zeros_like(stack_odd)

    def put_split(slot, value):
        high, low = split_two(value)
        gsplit[slot, 0 : 2 * rows] = high
        gsplit[slot, 2 * rows : 4 * rows] = low

    put_split(0, gcur[...])
    for o in range(1, nb):
        firsts[o - 1].wait_recv()
        setup(bl_peer(o))

    def gather(slot, off, width):
        both = jnp.dot(
            gsplit[slot], table[:, pl.ds(off, width)], preferred_element_type=f32
        )
        return both[: 2 * rows] + both[2 * rows :]

    def fold(value):
        value = value[:8] + value[8:]
        shift = fl
        while shift < 8:
            value = value + pltpu.roll(value, shift, 0)
            shift *= 2
        return value

    def model(left, right, sub, field, cols):
        inside = slice(sub * 128, (sub + 1) * 128)
        real, imag = [None] * slots, [None] * slots
        for w in range(units):
            re, im = slice(w * 16, w * 16 + 16), slice(rows + w * 16, rows + w * 16 + 16)
            lr, li = left[re, inside], left[im, inside]
            rr, ri = right[re, inside], right[im, inside]
            pr = lr * rr + li * ri
            pi = li * rr - lr * ri
            for t in range(slots):
                sr, si = field(0, t, re, cols), field(1, t, re, cols)
                mr, mi = pr * sr - pi * si, pr * si + pi * sr
                real[t] = mr if w == 0 else real[t] + mr
                imag[t] = mi if w == 0 else imag[t] + mi
        return [fold(v) for v in real], [fold(v) for v in imag]

    def sky_all(c, t, at, cols):
        return sky[c, t, at, cols]

    sides = (side_even, side_odd)

    def gather_part(n):
        at = n * width
        here = slice(n // 2 * width, n // 2 * width + width)
        for s in range(2):
            sides[n % 2][s, :, here] = gather(0, s * total + at, width)

    def predict(observed):
        misfit = jnp.zeros((8, 128), f32)
        for n in range(total // width + 1):
            if n < total // width:
                gather_part(n)
            if n == 0:
                continue
            at = (n - 1) * width
            here = slice((n - 1) // 2 * width, (n - 1) // 2 * width + width)
            left, right = sides[(n - 1) % 2].at[0, :, here], sides[(n - 1) % 2].at[1, :, here]
            for sub in range(width // 128):
                cols = pl.ds(at + sub * 128, 128)
                real, imag = model(left, right, sub, sky_all, cols)
                for t in range(slots):
                    if observed:
                        real[t] = visd[0, t, :, cols] - real[t]
                        imag[t] = visd[1, t, :, cols] - imag[t]
                        power = real[t] * real[t] + imag[t] * imag[t]
                        misfit = misfit + flagd[t, :, cols] * power
                    err[0, t, :, cols] = real[t]
                    err[1, t, :, cols] = imag[t]
        return misfit

    def folded(value):
        value = jnp.sum(value, axis=0, keepdims=True) * (1.0 / kp)
        return value + pltpu.roll(value, 64, 1)

    def put_misfit(it, value):
        sbuf[it, 0] = jnp.where(lane < 64, folded(value), fixed[...])

    def put_count(value):
        value = folded(value)
        value = value + pltpu.roll(value, 32, 1)
        fixed[...] = jnp.where((lane >= 64) & (lane < 96), value, gram_row)

    def lanes_sum(value, start, stop):
        inside = (lane >= start) & (lane < stop)
        return jnp.sum(jnp.where(inside, value, 0.0), axis=1, keepdims=True)

    predict(False)
    if paired:
        build_twin(0, nb // 2)
    for copy in seconds:
        copy.wait_recv()

    def spread_rows(value):
        return jnp.concatenate([value] * kp, axis=0)

    def observe():
        def outer(g, sums):
            def step(i, sums):
                misfit, count = sums
                here = pl.ds(pl.multiple_of(i * 128, 128), 128)
                cols = pl.ds(pl.multiple_of(g * base + i * 128, 128), 128)
                for t in range(slots):
                    at = (2 * slots + t) * fl
                    weight = spread_rows(xin[g, at : at + fl, here])
                    flagd[t, :, cols] = weight
                    count = count + weight
                    power = None
                    for c in range(2):
                        at = (c * slots + t) * fl
                        seen = spread_rows(xin[g, at : at + fl, here])
                        visd[c, t, :, cols] = seen
                        value = seen - err[c, t, :, cols]
                        err[c, t, :, cols] = value
                        power = value * value if c == 0 else power + value * value
                    misfit = misfit + weight * power
                return misfit, count

            return blocks(base, 4, step, sums)

        zero = jnp.zeros((8, 128), f32)
        return lax.fori_loop(0, nb, outer, (zero, zero))

    def wait_all(ref, send, recv):
        return remote(ref, ref, send, recv, any_peer(1))

    def build_own_sky():
        for g in range(nb):
            def coord(t, cols):
                return coords[0, t : t + 1, cols], coords[1, t : t + 1, cols]

            def put(t, at, i, re, im, g=g):
                cols = pl.ds(pl.multiple_of(i * 128, 128), 128)
                sky_own[g, 0, t, at, cols] = re
                sky_own[g, 1, t, at, cols] = im

            build_sky(g, coord, put)

    def prepare_end():
        lanes_of = lax.broadcasted_iota(i32, (8 * dirn, 2 * rows), 1)
        rows_of = lax.broadcasted_iota(i32, (8 * dirn, 2 * rows), 0)
        ratio_lanes = by(lanes_of % fl, fl, lambda f: ratio[0, me * fl + f])
        basis = legendre(ratio_lanes)
        place = rows_of % 8
        value = jnp.zeros((8 * dirn, 2 * rows), f32)
        for c in range(2):
            for j in range(NPOLY):
                hit = (place == c * NPOLY + j) & (lanes_of // rows == c)
                hit = hit & ((lanes_of % rows) // fl == rows_of // 8)
                value = jnp.where(hit, basis[j], value)
        weights[...] = value
        chan = lax.broadcasted_iota(i32, (chans, 128), 0)
        basis = legendre(by(chan, chans, lambda f: ratio[0, f]))
        for j in range(NPOLY):
            pack[pack.shape[0] - 1, :, j * 128 : (j + 1) * 128] = basis[j]
        for c in range(2):
            for k in range(dirn):
                put = c * rows + k * fl
                dual_own[put : put + fl] = own_rows(dual, c, k)

    def iteration(it, carry):
        @pl.when(it == 0)
        def _():
            misfit, count = observe()
            put_count(count)
            put_misfit(it, misfit)

        @pl.when(it > 0)
        def _():
            put_misfit(it, predict(True))

        for o in reversed(range(1, ndev)):
            remote(
                sbuf.at[it, 0], sbuf.at[it, o], s_send.at[it], s_recv.at[it], any_peer(o)
            ).start()

        if paired:
            pl.when(it == 0)(lambda: build_twin(nb // 2, nb))
        pl.when(it == 1)(build_own_sky)
        pl.when(it == 2)(prepare_end)

        finish = wait_all(sbuf.at[it, pl.ds(1, ndev - 1)], s_send.at[it], s_recv.at[it])
        finish.wait_recv()
        sums = jnp.sum(sbuf[it], axis=0)
        sigma_sq = lanes_sum(sums, 0, 64) / (lanes_sum(sums, 64, 96) + 1.0) + small_term
        inverse = 1.0 / sigma_sq
        acc[...] = jnp.zeros_like(acc)

        def normal(n):
            at = n * part
            side, stacked = sides[at // width % 2], stacks[n % 2]
            for sub in range(part // 128):
                cols = pl.ds(at + sub * 128, 128)
                here = pl.ds(at // width // 2 * width + at % width + sub * 128, 128)
                weighted, wsum = [], None
                for t in range(slots):
                    er, ei = err[0, t, :, cols], err[1, t, :, cols]
                    power = er * er + ei * ei
                    r = flagd[t, :, cols] * (robust_dof + 1.0) / (robust_dof + power * inverse)
                    weighted.append([jnp.concatenate([r * e, r * e], axis=0) for e in (er, ei)])
                    wsum = r if t == 0 else wsum + r
                wsum = jnp.concatenate([wsum, wsum], axis=0)
                for w in range(units):
                    re, im = slice(w * 16, w * 16 + 16), slice(rows + w * 16, rows + w * 16 + 16)
                    lr, li = side[0, re, here], side[0, im, here]
                    rr, ri = side[1, re, here], side[1, im, here]
                    c2 = const[3, re] * wsum
                    xr = (lr * rr + li * ri) * c2
                    xi = (li * rr - lr * ri) * c2
                    for t in range(slots):
                        sr, si = sky[0, t, re, cols], sky[1, t, re, cols]
                        wr, wi = weighted[t]
                        xr = xr + (sr * wr + si * wi)
                        xi = xi + (sr * wi - si * wr)
                    terms = (
                        (rr * xr - ri * xi, lr * xr + li * xi),
                        (rr * xi + ri * xr, li * xr - lr * xi),
                        ((rr * rr + ri * ri) * c2, (lr * lr + li * li) * c2),
                    )
                    for q in range(3):
                        for s in range(2):
                            high, low = split_two(terms[q][s])
                            put = q * rows + w * 16
                            where = slice(s * part + sub * 128, s * part + sub * 128 + 128)
                            stacked[put : put + 16, where] = high
                            stacked[half + put : half + put + 16, where] = low

        def add_up(n):
            at, stacked = n * part, stacks[n % 2]
            if paired:
                acc[...] += jnp.dot(
                    stacked[...],
                    twin[2 * at : 2 * at + 2 * part, :],
                    preferred_element_type=f32,
                )
                return
            for s in range(2):
                acc[...] += lax.dot_general(
                    table[:, s * total + at : s * total + at + part],
                    stacked[:, s * part : (s + 1) * part],
                    (((1,), (1,)), ((), ())),
                    preferred_element_type=f32,
                )

        stacks = (stack_even, stack_odd)
        count = total // part
        for n in range(count + 1):
            if n > 0:
                add_up(n - 1)
            if n < count:
                normal(n)
        if paired:
            normals = acc[:half] + acc[half:]
        else:
            normals = (acc[:, :half] + acc[:, half:]).T
        divisor = 1.0 / (normals[2 * rows : 3 * rows] + wide(const[2]))
        for c in range(2):
            at = slice(c * rows, (c + 1) * rows)
            gcur[at] = 0.5 * (gcur[at] + (normals[at] + anchor[at]) * divisor)
        put_split(0, gcur[...])
        finish.wait_send()
        return carry

    lax.fori_loop(0, ITERS, iteration, 0)

    both = gcur[...] + dual_own[...]
    rhs[...] = jnp.dot(
        weights[...], both, preferred_element_type=f32, precision=lax.Precision.HIGHEST
    )

    def tile(ref, n):
        return ref.at[
            pl.ds(pl.multiple_of((n // lanes) * 8, 8), 8),
            pl.ds(pl.multiple_of((n % lanes) * 128, 128), 128),
        ]

    def tile_value(ref, n):
        return ref[
            pl.ds(pl.multiple_of((n // lanes) * 8, 8), 8),
            pl.ds(pl.multiple_of((n % lanes) * 128, 128), 128),
        ]

    def owning(n, action):
        if ndev <= chunks:
            action()
        else:
            pl.when(n < chunks)(action)

    def ident_of(o):
        peer = any_peer(o)
        return peer["bl"] * nf + peer["freq"]

    for o in reversed(range(1, ndev)):
        n = ident_of(o)

        def send(o=o, n=n):
            remote(
                tile(rhs, n), rsum.at[o], c_send.at[0], c_recv.at[0], any_peer(o)
            ).start()

        owning(n, send)

    gall[me] = gcur[...]
    spread = [
        remote(gall.at[me], gall.at[me], g_send.at[o], g_recv.at[o], {"bl": bl_peer(o)})
        for o in range(1, nb)
    ]
    for copy in spread:
        copy.start()

    def residual(o):
        g = bl_peer(o)
        if o > 0:
            spread[o - 1].wait_recv()
            put_split(0, gall[g])

        def sky_here(c, t, at, cols):
            return sky_own[g, c, t, at, cols]

        sides = []
        for at in range(0, base, ch):
            off = me * base + at
            sides.append(
                (gather(0, pl.multiple_of(off, ch), ch), gather(0, pl.multiple_of(total + off, ch), ch))
            )
        for n, (left, right) in enumerate(sides):
            for sub in range(ch // 128):
                cols = pl.ds(n * ch + sub * 128, 128)
                parts = model(left, right, sub, sky_here, cols)
                for c in range(2):
                    for t in range(slots):
                        put = (c * slots + t) * fl
                        resbuf[g, put : put + fl, cols] = (
                            sendx[g, put : put + fl, cols] - parts[c][t][:fl]
                        )

    residual(0)

    gram_total = jnp.sum(sbuf[0], axis=0)
    gram = {
        ab: lanes_sum(gram_total, 96 + n, 97 + n)
        for n, ab in enumerate(GRAMS)
    }
    factor = {}
    for a in range(NPOLY):
        for b in range(a + 1):
            value = gram[a, b]
            for m in range(b):
                value = value - factor[a, m] * factor[b, m]
            factor[a, b] = jnp.sqrt(value) if a == b else value / factor[b, b]

    def solve():
        wait_all(rsum.at[pl.ds(1, ndev - 1)], c_send.at[2], c_recv.at[0]).wait_recv()
        rsum[0] = tile_value(rhs, ident)
        part = jnp.sum(rsum[...], axis=0)
        for c in range(2):
            forward = []
            for a in range(NPOLY):
                running = part[c * NPOLY + a : c * NPOLY + a + 1]
                for b in range(a):
                    running = running - factor[a, b] * forward[b]
                forward.append(running / factor[a, a])
            backward = [None] * NPOLY
            for a in reversed(range(NPOLY)):
                running = forward[a]
                for b in range(a + 1, NPOLY):
                    running = running - factor[b, a] * backward[b]
                backward[a] = running / factor[a, a]
            for j in range(NPOLY):
                solved[c * NPOLY + j : c * NPOLY + j + 1] = backward[j]
        for at in range(2 * NPOLY, 8):
            solved[at : at + 1] = jnp.zeros((1, 128), f32)
        coef[
            pl.ds(pl.multiple_of((ident // lanes) * 8, 8), 8),
            pl.ds(pl.multiple_of((ident % lanes) * 128, 128), 128),
        ] = solved[...]
        for o in reversed(range(1, ndev)):
            remote(
                solved, tile(coef, ident), c_send.at[1], c_recv.at[1], any_peer(o)
            ).start()

    owning(ident, solve)

    for o in range(1, nb):
        residual(o)

    for g in range(nb):
        own = slice(g * fl, (g + 1) * fl)
        for c in range(2):
            for t in range(slots):
                put = (c * slots + t) * fl
                for q in range(base // stations):
                    spot = 2 * dirn + (c * slots + t) * (base // stations) + q
                    pack[spot, own] = resbuf[g, put : put + fl, q * stations : (q + 1) * stations]
            for k in range(dirn):
                put = c * rows + k * fl
                pack[c * dirn + k, own] = gall[g, put : put + fl]

    def wait_tiles(count, send, recv, what):
        waiter = wait_all(rsum.at[pl.ds(0, count)], send, recv)
        if what == "send":
            waiter.wait_send()
        else:
            waiter.wait_recv()

    if ndev <= chunks:
        wait_tiles(ndev - 1, c_send.at[1], c_recv.at[1], "recv")
    else:
        @pl.when(ident < chunks)
        def _():
            wait_tiles(chunks - 1, c_send.at[1], c_recv.at[1], "recv")

        @pl.when(ident >= chunks)
        def _():
            wait_tiles(chunks, c_send.at[1], c_recv.at[1], "recv")

    spot = 2 * dirn + 2 * slots * (base // stations)
    for n in range(8 * dirn // chans):
        pack[spot + n] = coef[n * chans : (n + 1) * chans]

    if ndev <= chunks:
        wait_tiles(ndev - 1, c_send.at[0], c_recv.at[0], "send")
        wait_tiles(ndev - 1, c_send.at[1], c_recv.at[1], "send")
    else:
        @pl.when(ident < chunks)
        def _():
            wait_tiles(chunks - 1, c_send.at[0], c_recv.at[0], "send")
            wait_tiles(ndev - 1, c_send.at[1], c_recv.at[1], "send")

        @pl.when(ident >= chunks)
        def _():
            wait_tiles(chunks, c_send.at[0], c_recv.at[0], "send")

    for copy in firsts + seconds + spread:
        copy.wait_send()


def finish_kernel(sizes, pack, dual, gains_out, cons_out, dual_out, resid_out, cons, new_dual, sems):
    slots, chans, base, dirn, stations = sizes
    wide = base // stations
    copies = []

    def send(src, dst):
        copies.append(pltpu.make_async_copy(src, dst, sems.at[len(copies)]))
        copies[-1].start()

    for c in range(2):
        for t in range(slots):
            for q in range(wide):
                spot = 2 * dirn + (c * slots + t) * wide + q
                send(pack.at[spot], resid_out.at[c, t, :, pl.ds(q * stations, stations)])
        send(pack.at[pl.ds(c * dirn, dirn)], gains_out.at[c])
    last = pack.shape[0] - 1
    basis = [
        jnp.broadcast_to(pack[last, :, j * 128 : j * 128 + 1], (chans, stations))
        for j in range(NPOLY)
    ]
    spot = 2 * dirn + 2 * slots * wide
    for c in range(2):
        for k in range(dirn):
            value = dual[c, k] + pack[c * dirn + k]
            for j in range(NPOLY):
                put = k * 8 + c * NPOLY + j
                coefficient = pack[spot + put // chans, put % chans : put % chans + 1]
                cons[c, j, k : k + 1] = coefficient
                value = value - basis[j] * coefficient
            new_dual[c, k] = value
        send(new_dual.at[c], dual_out.at[c])
    send(cons, cons_out)
    for copy in copies:
        copy.wait()


def body(nb, nf, vis, flag, pair, coords, dirs, flux, ratio, gains, dual, cons, penalty):
    _, slots, chans, base = vis.shape
    dirn, stations = gains.shape[1], gains.shape[3]
    fl = chans // nb
    rows = dirn * fl
    total = base * nb
    ndev = nb * nf
    ch = chunk_of(stations, total, base)
    paired = fits_twice(stations, total)
    half = 3 * rows if paired else 128 * (-(-3 * rows // 128))
    ratio = ratio.reshape(1, -1)
    rho_scale = 2.0 * total * slots / stations
    sizes = (nb, nf, slots, chans, base, dirn, stations, rho_scale)
    vmem = pl.BlockSpec(memory_space=pltpu.VMEM)
    smem = pl.BlockSpec(memory_space=pltpu.SMEM)
    dma = pltpu.SemaphoreType.DMA
    shape = jax.ShapeDtypeStruct
    wide = base // stations
    blocks_out = 2 * dirn + 2 * slots * wide + 8 * dirn // chans + 1
    (pack,) = pl.pallas_call(
        functools.partial(kernel, sizes),
        name="admm_step",
        out_shape=(
            shape((blocks_out, chans, stations), f32),
        ),
        in_specs=[vmem, vmem, vmem, vmem, smem, smem, smem, vmem, vmem, vmem, smem],
        out_specs=(vmem,),
        scratch_shapes=[
            pltpu.VMEM((stations, 2 * total), bf16),
            pltpu.VMEM((2 * total, stations) if paired else (16, 128), bf16),
            pltpu.VMEM((nb, 2 + 2 * slots, base), f32),
            pltpu.VMEM((nb, 3 * slots * fl, base), f32),
            pltpu.VMEM((nb, 3 * slots * fl, base), f32),
            pltpu.VMEM((2, slots, rows, total), f32),
            pltpu.VMEM((nb, 2, slots, rows, base), f32),
            pltpu.VMEM((4, rows, 128), f32),
            pltpu.VMEM((nb, 2, rows, 128), f32),
            pltpu.VMEM((2 * rows, stations), f32),
            pltpu.VMEM((2, 2 * rows, total // 2), f32),
            pltpu.VMEM((2, 2 * rows, total // 2), f32),
            pltpu.VMEM((1, 4 * rows, stations), bf16),
            pltpu.VMEM((2 * rows, stations), f32),
            pltpu.VMEM((2, slots, 8, total), f32),
            pltpu.VMEM((slots, 8, total), f32),
            pltpu.VMEM((2, slots, 8, total), f32),
            pltpu.VMEM((2 * half, 2 * part_of(ch)), bf16),
            pltpu.VMEM((2 * half, 2 * part_of(ch)), bf16),
            pltpu.VMEM((2 * half, stations) if paired else (stations, 2 * half), f32),
            pltpu.VMEM((nb, 2 * rows, stations), f32),
            pltpu.VMEM((nb, 2 * slots * fl, base), f32),
            pltpu.VMEM((ITERS, ndev, 1, 128), f32),
            pltpu.VMEM((1, 128), f32),
            pltpu.VMEM((8 * dirn, stations), f32),
            pltpu.VMEM((ndev, 8, 128), f32),
            pltpu.VMEM((8, 128), f32),
            pltpu.VMEM((8 * dirn, stations), f32),
            pltpu.VMEM((8 * dirn, 2 * rows), f32),
            pltpu.VMEM((2 * rows, stations), f32),
            dma((nb,)),
            dma((nb,)),
            dma((nb,)),
            dma((nb,)),
            dma((ITERS,)),
            dma((ITERS,)),
            dma((nb,)),
            dma((nb,)),
            dma((3,)),
            dma((3,)),
        ],
        compiler_params=pltpu.CompilerParams(
            collective_id=0, has_side_effects=True, vmem_limit_bytes=(60 if paired else 63) * 1024 * 1024
        ),
    )(vis, flag, pair, coords, dirs, flux, ratio, gains, dual, cons, penalty)
    anywhere = pl.BlockSpec(memory_space=pl.ANY)
    return pl.pallas_call(
        functools.partial(finish_kernel, (slots, chans, base, dirn, stations)),
        name="finish",
        out_shape=(
            shape(gains.shape, f32),
            shape(cons.shape, f32),
            shape(dual.shape, f32),
            shape(vis.shape, f32),
        ),
        in_specs=[vmem, vmem],
        out_specs=(anywhere, anywhere, anywhere, anywhere),
        scratch_shapes=[
            pltpu.VMEM(cons.shape, f32),
            pltpu.VMEM(dual.shape, f32),
            dma((2 * slots * wide + 5,)),
        ],
        compiler_params=pltpu.CompilerParams(vmem_limit_bytes=16 * 1024 * 1024),
    )(pack, dual)


def solution(mesh):
    in_specs = (
        P(None, None, "freq", "bl"),
        P(None, "freq", "bl"),
        P(None, "bl"),
        P(None, None, "bl"),
        P(),
        P(None, "freq"),
        P("freq"),
        P(None, None, "freq", None),
        P(None, None, "freq", None),
        P(),
        P(),
    )
    out_specs = (
        P(None, None, "freq", None),
        P(),
        P(None, None, "freq", None),
        P(None, None, "freq", "bl"),
    )
    step = functools.partial(body, mesh.shape["bl"], mesh.shape["freq"])
    return jax.shard_map(step, mesh=mesh, in_specs=in_specs, out_specs=out_specs, check_vma=False)
```
